512 devices in a mesh: stream: 8 (over z), span: 16 (over y, core), depth: 4 (over x).
Axes of the slice: x: 4, y: 8, z: 8, core: 2. Of those that a mesh axis runs over, the one named last changes fastest.
Arguments:
- forward_velocity: float32 [3, 64, 256, 512], P(None, 'stream', 'span', 'depth'), may hold values from -40 to 40, as said below
- adjoint_velocity: float32 [3, 64, 256, 512], P(None, 'stream', 'span', 'depth'), may hold values from -40 to 40, as said below
- weights: float32 [32, 81], replicated, may hold values from -0.625 to 0.625
Outputs:
- basis: float32 [32, 64, 256, 512], P(None, 'stream', 'span', 'depth')
The draws below stay inside these ranges and needn't reach their ends.
Inputs may be any that keep to these rules, and one draw needn't show every extreme that they name: `forward_velocity`: a velocity field whose amplitude varies from cell to cell. `adjoint_velocity`: a velocity field whose amplitude varies from cell to cell.
All inputs are finite; a program needn't handle non-finite values.
Results may differ from the reference program's by a relative error of at most 0.0003.
Values sent between devices are 32-bit elements; how exact they have to be, the bound alone decides.
No kernel may reach another device: no remote copies, remote signals or barrier semaphores. Data moves between devices by JAX's collectives and lax.ppermute only.
A program may use at most 64 MiB of HBM per device.

```python
import jax
import jax.numpy as jnp
from jax import lax

CX = 8
NSNAP = 32
PAIRS = 81
NX = 64
NY = 256
NZ = 512
CELLS = 8388608


def velocity_field(key):
    base_key, scale_key = jax.random.split(key)
    shape = (3, NX, NY, NZ)
    unit = jax.random.uniform(scale_key, (1, NX, NY, NZ), jnp.float32)
    pos_x = jnp.arange(NX, dtype=jnp.float32)[:, None, None] / NX
    pos_y = jnp.arange(NY, dtype=jnp.float32)[None, :, None] / NY
    pos_z = jnp.arange(NZ, dtype=jnp.float32)[None, None, :] / NZ
    position = (pos_x + pos_y + pos_z)[None]
    values = jnp.clip(jax.random.normal(base_key, shape, jnp.float32), -4.0, 4.0)
    amplitude = jnp.exp(jnp.log(10.0) * unit - 1.15) * jnp.exp(0.25 * jnp.log(3.0) * position)
    return (values * amplitude).astype(jnp.float32)


def draw_forward_velocity(key, part):
    return velocity_field(jax.random.fold_in(key, 101))


def draw_adjoint_velocity(key, part):
    return velocity_field(jax.random.fold_in(key, 202))


def normal_values(stream_key, dims, width, most, kind=jnp.bfloat16):
    array = jax.random.normal(stream_key, dims, jnp.float32) * width
    return jnp.minimum(jnp.maximum(array, -most), most).astype(kind)


def setup_inputs(seed: int = 0) -> dict:
    key_of = jax.random.split(jax.random.key(seed), 4)
    forward_velocity = draw_forward_velocity(jax.random.fold_in(key_of[3], 71), 0)
    adjoint_velocity = draw_adjoint_velocity(jax.random.fold_in(key_of[3], 71), 0)
    weights = normal_values(key_of[2], (NSNAP, PAIRS), PAIRS ** -0.5, 0.625, jnp.float32)
    return dict(forward_velocity=forward_velocity, adjoint_velocity=adjoint_velocity, weights=weights)


def shifted(field, axis, offset):
    parts = [slice(None), slice(2, -2), slice(2, -2), slice(2, -2)]
    length = field.shape[axis]
    parts[axis] = slice(2 + offset, length - 2 + offset)
    return field[tuple(parts)]

def gradients(padded):
    slopes = []
    for axis in (1, 2, 3):
        near = shifted(padded, axis, 1) - shifted(padded, axis, -1)
        far = shifted(padded, axis, 2) - shifted(padded, axis, -2)
        slopes.append((8.0 * near - far) / 12.0)
    stacked = jnp.stack(slopes, axis=1)
    return stacked.reshape(stacked.shape[0] * 3, -1)

def snapshots(padded, weights):
    grads = gradients(padded)
    products = (grads[:9][:, None, :] * grads[9:][None, :, :]).reshape(81, -1)
    return jnp.dot(weights.astype(jnp.float32), products.astype(jnp.float32), precision=lax.Precision.HIGHEST, preferred_element_type=jnp.float32)

def reference(forward_velocity, adjoint_velocity, weights):
    stacked = jnp.concatenate([forward_velocity, adjoint_velocity], 0)
    padded = jnp.pad(stacked, ((0, 0), (2, 2), (2, 2), (2, 2)), mode='wrap')
    blocks = NX // CX

    def one_block(index):
        start = (index * CX).astype(jnp.int32)
        piece = lax.dynamic_slice_in_dim(padded, start, CX + 4, 1)
        return snapshots(piece, weights)
    snaps = lax.map(one_block, jnp.arange(blocks, dtype=jnp.int32))

    def block_gram(block):
        return jnp.dot(block.astype(jnp.float32), block.T.astype(jnp.float32), precision=lax.Precision.HIGHEST, preferred_element_type=jnp.float32)
    gram = jnp.sum(lax.map(block_gram, snaps), axis=0)
    lower = jnp.linalg.cholesky(gram / CELLS)
    inverse = jax.scipy.linalg.solve_triangular(lower, jnp.eye(NSNAP, dtype=jnp.float32), lower=True)

    def block_basis(block):
        return jnp.dot(inverse.astype(jnp.float32), block.astype(jnp.float32), precision=lax.Precision.HIGHEST, preferred_element_type=jnp.float32)
    basis = lax.map(block_basis, snaps)
    basis = basis.reshape(blocks, NSNAP, CX, NY, NZ).transpose(1, 0, 2, 3, 4)
    return basis.reshape(NSNAP, NX, NY, NZ)
```

```python
import functools

import jax
import jax.numpy as jnp
from jax import lax
from jax.experimental import pallas as pl
from jax.experimental.pallas import tpu as pltpu
from jax.sharding import PartitionSpec as P

F32 = jnp.float32
BF16 = jnp.bfloat16
INTERPRET = False
VMEM = pl.BlockSpec(memory_space=pltpu.VMEM)
GROUP = 82 * 8
DEPTH = 2048


def iota(shape, dim):
    return lax.broadcasted_iota(jnp.int32, shape, dim)


def split(value):
    high = value.astype(BF16)
    low = (value - high.astype(F32)).astype(BF16)
    return high, low


def dot(left, right):
    return jnp.dot(left, right, preferred_element_type=F32)


def dot_nt(left, right):
    return lax.dot_general(left, right, (((1,), (1,)), ((), ())), preferred_element_type=F32)


def place(index):
    return divmod(index * 4, 128)


def sends_kernel(f_ref, a_ref, xf, xl, yf, yl, zs):
    planes, rows = f_ref.shape[1], f_ref.shape[2]
    for ref, base in ((f_ref, 0), (a_ref, 3)):
        part = slice(base, base + 3)
        xf[part] = ref[:, 0:2]
        xl[part] = ref[:, planes - 2 : planes]
        yf[part] = ref[:, :, 0:2, :]
        yl[part] = ref[:, :, rows - 2 : rows, :]
    lane = iota((8, 128), 1)
    packed = [jnp.zeros((8, 128), F32) for _ in range(zs.shape[0] // 8)]
    for comp in range(6):
        ref = f_ref if comp < 3 else a_ref
        for plane in range(planes):
            for half in range(rows // 8):
                group, at = place((comp * planes + plane) * (rows // 8) + half)
                tile = ref[comp % 3, plane, 8 * half : 8 * half + 8, :]
                moved = pltpu.roll(tile, (2 + at) % 128, 1)
                here = (lane >= at) & (lane < at + 4)
                packed[group] = jnp.where(here, moved, packed[group])
    for group, tile in enumerate(packed):
        zs[8 * group : 8 * group + 8, :] = tile


def weights_kernel(w_ref, wk_ref):
    pairs = w_ref.shape[1]
    high, low = split(w_ref[...] * (1.0 / 144.0))
    q = iota((pairs, DEPTH), 1)
    p = iota((pairs, DEPTH), 0)
    r = jnp.where(q >= GROUP, q - GROUP, q)
    r = jnp.where(r >= GROUP, r - GROUP, r)
    hit = lax.shift_right_logical(r, 3) == p
    to_high = jnp.where(hit & (q < 2 * GROUP), 1.0, 0.0).astype(BF16)
    to_low = jnp.where(hit & (q >= 2 * GROUP) & (q < 3 * GROUP), 1.0, 0.0).astype(BF16)
    wide = (dot(high, to_high) + dot(low, to_low)).astype(BF16)
    wk_ref[...] = spread(wide)


def spread(wide):
    snaps, n = wide.shape
    rows = 8 * snaps
    e = (lax.shift_right_logical(iota((rows, snaps), 0), 3) == iota((rows, snaps), 1))
    tall = dot(jnp.where(e, 1.0, 0.0).astype(BF16), wide)
    same = (iota((rows, n), 0) & 7) == (iota((rows, n), 1) & 7)
    return jnp.where(same, tall, 0.0).astype(BF16)


def compute_kernel(f_ref, a_ref, xb, xa, yb, ya, zb, za, wk_ref, sh_ref, sl_ref, g_ref, ypad):
    planes, rows = f_ref.shape[1], f_ref.shape[2]
    halves = rows // 8
    lane = iota((8, 128), 1)
    total = None
    for comp in range(6):
        ref = f_ref if comp < 3 else a_ref
        for plane in range(planes):
            ypad[comp, plane, 8 : 8 + rows, :] = ref[comp % 3, plane]
    ypad[:, :, 6:8, :] = yb[...]
    ypad[:, :, 8 + rows : 10 + rows, :] = ya[...]

    def line(comp, plane):
        if plane < 0:
            return xb[comp, plane + 2]
        if plane >= planes:
            return xa[comp, plane - planes]
        return (f_ref if comp < 3 else a_ref)[comp % 3, plane]

    def depth_slope(comp, plane, half):
        tile = ypad[comp, plane, 8 + 8 * half : 16 + 8 * half, :]
        group, at = place((comp * planes + plane) * halves + half)
        before = zb[8 * group : 8 * group + 8, :]
        after = za[8 * group : 8 * group + 8, :]
        up1 = jnp.where(lane < 1, pltpu.roll(before, (127 - at) % 128, 1), pltpu.roll(tile, 1, 1))
        up2 = jnp.where(lane < 2, pltpu.roll(before, (128 - at) % 128, 1), pltpu.roll(tile, 2, 1))
        dn1 = jnp.where(lane >= 127, pltpu.roll(after, (125 - at) % 128, 1), pltpu.roll(tile, 127, 1))
        dn2 = jnp.where(lane >= 126, pltpu.roll(after, (124 - at) % 128, 1), pltpu.roll(tile, 126, 1))
        return 8.0 * (dn1 - up1) - (dn2 - up2)

    for plane in range(planes):
        slopes = []
        for comp in range(6):
            dx = 8.0 * (line(comp, plane + 1) - line(comp, plane - 1)) - (
                line(comp, plane + 2) - line(comp, plane - 2)
            )
            y = lambda k: ypad[comp, plane, 8 + k : 8 + k + rows, :]
            dy = 8.0 * (y(1) - y(-1)) - (y(2) - y(-2))
            dx = jnp.concatenate([dx[8 * h : 8 * h + 8] for h in range(halves)], 1)
            dy = jnp.concatenate([dy[8 * h : 8 * h + 8] for h in range(halves)], 1)
            dz = jnp.concatenate([depth_slope(comp, plane, h) for h in range(halves)], 1)
            slopes += [dx, dy, dz]
        products = [slopes[a] * slopes[9 + b] for a in range(9) for b in range(9)]
        products.append(jnp.zeros_like(products[0]))
        high, low = split(jnp.concatenate(products, 0))
        rest = jnp.zeros((DEPTH - 3 * GROUP, high.shape[1]), BF16)
        block = dot(wk_ref[...], jnp.concatenate([high, low, high, rest], 0))
        high, low = split(block)
        sh_ref[plane] = high
        sl_ref[plane] = low
        part = dot_nt(jnp.concatenate([high, low], 0), high)
        total = part if total is None else total + part

    n = total.shape[1]
    same = (iota((n, n), 0) & 7) == (iota((n, n), 1) & 7)
    main = jnp.where(same, total[:n] + total[n:], 0.0)
    cross = jnp.where(same, total[n:], 0.0).astype(BF16)
    snaps = n // 8
    et = jnp.where(
        lax.shift_right_logical(iota((snaps, n), 1), 3) == iota((snaps, n), 0), 1.0, 0.0
    )
    narrow = jnp.dot(et, main, precision=lax.Precision.HIGHEST, preferred_element_type=F32)
    narrow = narrow + dot_nt(et.astype(BF16), cross)
    tiled = jnp.where(
        lax.shift_right_logical(iota((n, 128), 0), 3) == (iota((n, 128), 1) & 31), 1.0, 0.0
    )
    gram = jnp.dot(narrow, tiled, precision=lax.Precision.HIGHEST, preferred_element_type=F32)
    packed = gram[0:8]
    for k in range(1, snaps // 8):
        packed = jnp.where(lane >= 32 * k, gram[8 * k : 8 * k + 8], packed)
    g_ref[...] = jnp.broadcast_to(packed[None], g_ref.shape)


def inverse_factor(gram, snaps):
    row, lane = iota(gram.shape, 0), iota(gram.shape, 1)
    work = jnp.where(lane < snaps, gram, jnp.where(lane == row + snaps, 1.0, 0.0))
    for k in range(snaps - 1):
        pivot = work[k : k + 1, k : k + 1]
        scaled = work[k : k + 1, :] * (1.0 / pivot)
        work = jnp.where(row > k, work - work[:, k : k + 1] * scaled, work)
    diagonal = jnp.sum(jnp.where(lane == row, work, 0.0), axis=1, keepdims=True)
    work = work * (1.0 / jnp.sqrt(diagonal))
    return jnp.where(lane < snaps, pltpu.roll(work, 128 - snaps, 1), 0.0)


def basis_kernel(cells, r_ref, sh_ref, sl_ref, o_ref, lk_ref):
    n = sh_ref.shape[1]
    snaps = n // 8

    @pl.when(pl.program_id(0) == 0)
    def _():
        packed = r_ref[0]
        for i in range(1, r_ref.shape[0]):
            packed = packed + r_ref[i]
        packed = packed * (1.0 / cells)
        gram = jnp.concatenate(
            [packed] + [pltpu.roll(packed, 128 - 32 * k, 1) for k in range(1, snaps // 8)], 0
        )
        high, low = split(inverse_factor(gram, snaps))
        to_wide = jnp.where(
            lax.shift_right_logical(iota((128, n), 1), 3) == iota((128, n), 0), 1.0, 0.0
        ).astype(BF16)
        high = spread(dot(high, to_wide).astype(BF16))
        low = spread(dot(low, to_wide).astype(BF16))
        lk_ref[:, 0:n] = high
        lk_ref[:, n : 2 * n] = high
        lk_ref[:, 2 * n : 3 * n] = low

    for plane in range(sh_ref.shape[0]):
        high = sh_ref[plane]
        out = dot(lk_ref[...], jnp.concatenate([high, sl_ref[plane], high], 0))
        for half in range(o_ref.shape[2] // 8):
            part = out[:, 128 * half : 128 * half + 128]
            o_ref[:, plane, 8 * half : 8 * half + 8, :] = part.reshape(snaps, 8, 128)


def shape(*dims, dtype=F32):
    return jax.ShapeDtypeStruct(dims, dtype)


def body(forward_velocity, adjoint_velocity, weights):
    _, planes, rows, cols = forward_velocity.shape
    snaps = weights.shape[0]
    n = 8 * snaps
    width = rows // 8 * cols
    zrows = -(-6 * planes * (rows // 8) * 4 // 128) * 8
    params = pltpu.CompilerParams(vmem_limit_bytes=48 * 2**20)

    xf, xl, yf, yl, zs = pl.pallas_call(
        sends_kernel,
        in_specs=[VMEM] * 2,
        out_specs=[VMEM] * 5,
        out_shape=[
            shape(6, 2, rows, cols),
            shape(6, 2, rows, cols),
            shape(6, planes, 2, cols),
            shape(6, planes, 2, cols),
            shape(zrows, 128),
        ],
        compiler_params=params,
        interpret=INTERPRET,
    )(forward_velocity, adjoint_velocity)

    def move(value, axis, step):
        size = lax.axis_size(axis)
        return lax.ppermute(value, axis, [(i, (i + step) % size) for i in range(size)])

    xb, xa = move(xl, "stream", 1), move(xf, "stream", -1)
    yb, ya = move(yl, "span", 1), move(yf, "span", -1)
    zb, za = move(zs, "depth", 1), move(zs, "depth", -1)

    wk = pl.pallas_call(
        weights_kernel,
        in_specs=[VMEM],
        out_specs=VMEM,
        out_shape=shape(n, DEPTH, dtype=BF16),
        compiler_params=params,
        interpret=INTERPRET,
    )(weights)

    span = lax.axis_size("span")
    others = lax.axis_size(("stream", "depth"))
    sh, sl, grams = pl.pallas_call(
        compute_kernel,
        in_specs=[VMEM] * 9,
        out_specs=[VMEM] * 3,
        out_shape=[
            shape(planes, n, width, dtype=BF16),
            shape(planes, n, width, dtype=BF16),
            shape(span, 8, 128),
        ],
        scratch_shapes=[pltpu.VMEM((6, planes, rows + 16, cols), F32)],
        compiler_params=params,
        interpret=INTERPRET,
    )(forward_velocity, adjoint_velocity, xb, xa, yb, ya, zb, za, wk)

    grams = lax.all_to_all(grams, "span", 0, 0, tiled=True)
    grams = jnp.broadcast_to(grams.sum(0)[None], (others, 8, 128))
    grams = lax.all_to_all(grams, ("stream", "depth"), 0, 0, tiled=True)

    cells = planes * rows * cols * span * others
    step = 2
    return pl.pallas_call(
        functools.partial(basis_kernel, cells),
        grid=(planes // step,),
        in_specs=[
            VMEM,
            pl.BlockSpec((step, n, width), lambda i: (i, 0, 0)),
            pl.BlockSpec((step, n, width), lambda i: (i, 0, 0)),
        ],
        out_specs=pl.BlockSpec((snaps, step, rows, cols), lambda i: (0, i, 0, 0)),
        out_shape=shape(snaps, planes, rows, cols),
        scratch_shapes=[pltpu.VMEM((n, 3 * n), BF16)],
        compiler_params=params,
        interpret=INTERPRET,
    )(grams, sh, sl)


def solution(mesh):
    spec = P(None, "stream", "span", "depth")
    return jax.shard_map(body, mesh=mesh, in_specs=(spec, spec, P()), out_specs=spec, check_vma=False)
```

```python
import functools

import jax
import jax.numpy as jnp
from jax import lax
from jax.experimental import pallas as pl
from jax.experimental.pallas import tpu as pltpu
from jax.sharding import PartitionSpec as P

F32 = jnp.float32
BF16 = jnp.bfloat16
INTERPRET = False
VMEM = pl.BlockSpec(memory_space=pltpu.VMEM)
HBM = pl.BlockSpec(memory_space=pltpu.HBM)
GROUP = 82 * 8
DEPTH = 2048
BLOCK = 8


def iota(shape, dim):
    return lax.broadcasted_iota(jnp.int32, shape, dim)


def split(value):
    high = value.astype(BF16)
    low = (value - high.astype(F32)).astype(BF16)
    return high, low


def dot(left, right):
    return jnp.dot(left, right, preferred_element_type=F32)


def dot_nt(left, right):
    return lax.dot_general(left, right, (((1,), (1,)), ((), ())), preferred_element_type=F32)


def place(index):
    return divmod(index * 4, 128)


def sends_kernel(f_hbm, a_hbm, w_hbm, fields, w_ref, xf, xl, yf, yl, zs, sems):
    copies = [
        pltpu.make_async_copy(f_hbm, fields.at[0:3], sems.at[0]),
        pltpu.make_async_copy(a_hbm, fields.at[3:6], sems.at[1]),
        pltpu.make_async_copy(w_hbm, w_ref, sems.at[2]),
    ]
    for copy in copies:
        copy.start()
    for copy in copies:
        copy.wait()
    comps, planes, rows = fields.shape[:3]
    xf[...] = fields[:, 0:2]
    xl[...] = fields[:, planes - 2 : planes]
    yf[...] = fields[:, :, 0:2, :]
    yl[...] = fields[:, :, rows - 2 : rows, :]
    lane = iota((8, 128), 1)
    packed = [jnp.zeros((8, 128), F32) for _ in range(zs.shape[0] // 8)]
    for comp in range(comps):
        for plane in range(planes):
            for half in range(rows // 8):
                group, at = place((comp * planes + plane) * (rows // 8) + half)
                tile = fields[comp, plane, 8 * half : 8 * half + 8, :]
                moved = pltpu.roll(tile, (2 + at) % 128, 1)
                here = (lane >= at) & (lane < at + 4)
                packed[group] = jnp.where(here, moved, packed[group])
    for group, tile in enumerate(packed):
        zs[8 * group : 8 * group + 8, :] = tile


def weights_kernel(w_ref, wk_ref):
    pairs = w_ref.shape[1]
    high, low = split(w_ref[...] * (1.0 / 144.0))
    q = iota((pairs, DEPTH), 1)
    p = iota((pairs, DEPTH), 0)
    r = jnp.where(q >= GROUP, q - GROUP, q)
    r = jnp.where(r >= GROUP, r - GROUP, r)
    hit = lax.shift_right_logical(r, 3) == p
    to_high = jnp.where(hit & (q < 2 * GROUP), 1.0, 0.0).astype(BF16)
    to_low = jnp.where(hit & (q >= 2 * GROUP) & (q < 3 * GROUP), 1.0, 0.0).astype(BF16)
    wide = (dot(high, to_high) + dot(low, to_low)).astype(BF16)
    wk_ref[...] = spread(wide)


def spread(wide):
    snaps, n = wide.shape
    rows = 8 * snaps
    e = (lax.shift_right_logical(iota((rows, snaps), 0), 3) == iota((rows, snaps), 1))
    tall = dot(jnp.where(e, 1.0, 0.0).astype(BF16), wide)
    same = (iota((rows, n), 0) & 7) == (iota((rows, n), 1) & 7)
    return jnp.where(same, tall, 0.0).astype(BF16)


def compute_kernel(fields, xb, xa, yb, ya, zb, za, wk_ref, sh_ref, sl_ref, g_ref, ypad):
    planes, rows = fields.shape[1], fields.shape[2]
    halves = rows // 8
    lane = iota((8, 128), 1)
    total = None
    ypad[:, :, 8 : 8 + rows, :] = fields[...]
    ypad[:, :, 6:8, :] = yb[...]
    ypad[:, :, 8 + rows : 10 + rows, :] = ya[...]

    def line(comp, plane):
        if plane < 0:
            return xb[comp, plane + 2]
        if plane >= planes:
            return xa[comp, plane - planes]
        return fields[comp, plane]

    def depth_slope(comp, plane, half):
        tile = fields[comp, plane, 8 * half : 8 * half + 8, :]
        group, at = place((comp * planes + plane) * halves + half)
        before = zb[8 * group : 8 * group + 8, :]
        after = za[8 * group : 8 * group + 8, :]
        up1 = jnp.where(lane < 1, pltpu.roll(before, (127 - at) % 128, 1), pltpu.roll(tile, 1, 1))
        up2 = jnp.where(lane < 2, pltpu.roll(before, (128 - at) % 128, 1), pltpu.roll(tile, 2, 1))
        dn1 = jnp.where(lane >= 127, pltpu.roll(after, (125 - at) % 128, 1), pltpu.roll(tile, 127, 1))
        dn2 = jnp.where(lane >= 126, pltpu.roll(after, (124 - at) % 128, 1), pltpu.roll(tile, 126, 1))
        return 8.0 * (dn1 - up1) - (dn2 - up2)

    for plane in range(planes):
        slopes = []
        for comp in range(6):
            dx = 8.0 * (line(comp, plane + 1) - line(comp, plane - 1)) - (
                line(comp, plane + 2) - line(comp, plane - 2)
            )
            y = lambda k: ypad[comp, plane, 8 + k : 8 + k + rows, :]
            dy = 8.0 * (y(1) - y(-1)) - (y(2) - y(-2))
            dx = jnp.concatenate([dx[8 * h : 8 * h + 8] for h in range(halves)], 1)
            dy = jnp.concatenate([dy[8 * h : 8 * h + 8] for h in range(halves)], 1)
            dz = jnp.concatenate([depth_slope(comp, plane, h) for h in range(halves)], 1)
            slopes += [dx, dy, dz]
        products = [slopes[a] * slopes[9 + b] for a in range(9) for b in range(9)]
        products.append(jnp.zeros_like(products[0]))
        high, low = split(jnp.concatenate(products, 0))
        rest = jnp.zeros((DEPTH - 3 * GROUP, high.shape[1]), BF16)
        block = dot(wk_ref[...], jnp.concatenate([high, low, high, rest], 0))
        high, low = split(block)
        sh_ref[plane] = high
        sl_ref[plane] = low
        part = dot_nt(jnp.concatenate([high, low], 0), high)
        total = part if total is None else total + part

    n = total.shape[1]
    same = (iota((n, n), 0) & 7) == (iota((n, n), 1) & 7)
    main = jnp.where(same, total[:n] + total[n:], 0.0)
    cross = jnp.where(same, total[n:], 0.0).astype(BF16)
    snaps = n // 8
    et = jnp.where(
        lax.shift_right_logical(iota((snaps, n), 1), 3) == iota((snaps, n), 0), 1.0, 0.0
    )
    narrow = jnp.dot(et, main, precision=lax.Precision.HIGHEST, preferred_element_type=F32)
    narrow = narrow + dot_nt(et.astype(BF16), cross)
    tiled = jnp.where(
        lax.shift_right_logical(iota((n, 128), 0), 3) == (iota((n, 128), 1) & 31), 1.0, 0.0
    )
    gram = jnp.dot(narrow, tiled, precision=lax.Precision.HIGHEST, preferred_element_type=F32)
    packed = gram[0:8]
    for k in range(1, snaps // 8):
        packed = jnp.where(lane >= 32 * k, gram[8 * k : 8 * k + 8], packed)
    g_ref[...] = jnp.broadcast_to(packed[None], g_ref.shape)


def inverse_factor(gram, snaps):
    row, lane = iota(gram.shape, 0), iota(gram.shape, 1)
    work = jnp.where(lane < snaps, gram, jnp.where(lane == row + snaps, 1.0, 0.0))
    for first in range(0, snaps, BLOCK):
        block = range(first, first + BLOCK)
        cols = [jnp.broadcast_to(work[:, k : k + 1], work.shape) for k in block]
        rows = [work[k : k + 1, :] for k in block]
        for i, k in enumerate(block):
            inverse = 1.0 / cols[i][k : k + 1, :]
            below = jnp.where(row > k, cols[i], 0.0)
            scaled = rows[i] * inverse
            work = work - below * scaled
            for j in range(i + 1, BLOCK):
                entry = cols[i][first + j : first + j + 1, :]
                cols[j] = cols[j] - below * (entry * inverse)
                rows[j] = rows[j] - entry * scaled
    diagonal = jnp.sum(jnp.where(lane == row, work, 0.0), axis=1, keepdims=True)
    work = work * (1.0 / jnp.sqrt(diagonal))
    return jnp.where(lane < snaps, pltpu.roll(work, 128 - snaps, 1), 0.0)


def basis_kernel(cells, r_ref, sh_ref, sl_ref, o_hbm, lk_ref, out_ref, sems):
    planes, n = sh_ref.shape[:2]
    snaps = n // 8
    packed = r_ref[0]
    for i in range(1, r_ref.shape[0]):
        packed = packed + r_ref[i]
    packed = packed * (1.0 / cells)
    gram = jnp.concatenate(
        [packed] + [pltpu.roll(packed, 128 - 32 * k, 1) for k in range(1, snaps // 8)], 0
    )
    high, low = split(inverse_factor(gram, snaps))
    to_wide = jnp.where(
        lax.shift_right_logical(iota((128, n), 1), 3) == iota((128, n), 0), 1.0, 0.0
    ).astype(BF16)
    high = spread(dot(high, to_wide).astype(BF16))
    low = spread(dot(low, to_wide).astype(BF16))
    lk_ref[:, 0:n] = high
    lk_ref[:, n : 2 * n] = high
    lk_ref[:, 2 * n : 3 * n] = low

    copies = []
    for plane in range(planes):
        high = sh_ref[plane]
        out = dot(lk_ref[...], jnp.concatenate([high, sl_ref[plane], high], 0))
        for half in range(out_ref.shape[2] // 8):
            part = out[:, 128 * half : 128 * half + 128]
            out_ref[plane, :, 8 * half : 8 * half + 8, :] = part.reshape(snaps, 8, 128)
        copy = pltpu.make_async_copy(out_ref.at[plane], o_hbm.at[:, plane], sems.at[plane])
        copy.start()
        copies.append(copy)
    for copy in copies:
        copy.wait()


def shape(*dims, dtype=F32):
    return jax.ShapeDtypeStruct(dims, dtype)


def body(forward_velocity, adjoint_velocity, weights):
    _, planes, rows, cols = forward_velocity.shape
    snaps = weights.shape[0]
    n = 8 * snaps
    width = rows // 8 * cols
    zrows = -(-6 * planes * (rows // 8) * 4 // 128) * 8
    params = pltpu.CompilerParams(vmem_limit_bytes=48 * 2**20)

    fields, w, xf, xl, yf, yl, zs = pl.pallas_call(
        sends_kernel,
        in_specs=[HBM] * 3,
        out_specs=[VMEM] * 7,
        out_shape=[
            shape(6, planes, rows, cols),
            shape(*weights.shape),
            shape(6, 2, rows, cols),
            shape(6, 2, rows, cols),
            shape(6, planes, 2, cols),
            shape(6, planes, 2, cols),
            shape(zrows, 128),
        ],
        scratch_shapes=[pltpu.SemaphoreType.DMA((3,))],
        compiler_params=params,
        interpret=INTERPRET,
    )(*(pltpu.with_memory_space_constraint(x, pltpu.HBM) for x in (forward_velocity, adjoint_velocity, weights)))

    def move(value, axis, step):
        size = lax.axis_size(axis)
        return lax.ppermute(value, axis, [(i, (i + step) % size) for i in range(size)])

    xb, xa = move(xl, "stream", 1), move(xf, "stream", -1)
    yb, ya = move(yl, "span", 1), move(yf, "span", -1)
    zb = move(lax.optimization_barrier((zs, xb))[0], "depth", 1)
    za = move(lax.optimization_barrier((zs, xa))[0], "depth", -1)

    wk = pl.pallas_call(
        weights_kernel,
        in_specs=[VMEM],
        out_specs=VMEM,
        out_shape=shape(n, DEPTH, dtype=BF16),
        compiler_params=params,
        interpret=INTERPRET,
    )(w)

    span = lax.axis_size("span")
    others = lax.axis_size(("stream", "depth"))
    sh, sl, grams = pl.pallas_call(
        compute_kernel,
        in_specs=[VMEM] * 8,
        out_specs=[VMEM] * 3,
        out_shape=[
            shape(planes, n, width, dtype=BF16),
            shape(planes, n, width, dtype=BF16),
            shape(span, 8, 128),
        ],
        scratch_shapes=[pltpu.VMEM((6, planes, rows + 16, cols), F32)],
        compiler_params=params,
        interpret=INTERPRET,
    )(fields, xb, xa, yb, ya, zb, za, wk)

    grams = lax.all_to_all(grams, "span", 0, 0, tiled=True)
    grams = jnp.broadcast_to(grams.sum(0)[None], (others, 8, 128))
    grams = lax.all_to_all(grams, ("stream", "depth"), 0, 0, tiled=True)

    cells = planes * rows * cols * span * others
    return pl.pallas_call(
        functools.partial(basis_kernel, cells),
        in_specs=[VMEM] * 3,
        out_specs=HBM,
        out_shape=shape(snaps, planes, rows, cols),
        scratch_shapes=[
            pltpu.VMEM((n, 3 * n), BF16),
            pltpu.VMEM((planes, snaps, rows, cols), F32),
            pltpu.SemaphoreType.DMA((planes,)),
        ],
        compiler_params=params,
        interpret=INTERPRET,
    )(grams, sh, sl)


def solution(mesh):
    spec = P(None, "stream", "span", "depth")
    return jax.shard_map(body, mesh=mesh, in_specs=(spec, spec, P()), out_specs=spec, check_vma=False)
```

```python
import functools

import jax
import jax.numpy as jnp
from jax import lax
from jax.experimental import pallas as pl
from jax.experimental.pallas import tpu as pltpu
from jax.sharding import PartitionSpec as P

F32 = jnp.float32
BF16 = jnp.bfloat16
INTERPRET = False
VMEM = pl.BlockSpec(memory_space=pltpu.VMEM)
HBM = pl.BlockSpec(memory_space=pltpu.HBM)
GROUP = 80
DEPTH = 256
BLOCK = 8


def iota(shape, dim):
    return lax.broadcasted_iota(jnp.int32, shape, dim)


def split(value):
    high = value.astype(BF16)
    low = (value - high.astype(F32)).astype(BF16)
    return high, low


def dot(left, right):
    return jnp.dot(left, right, preferred_element_type=F32)


def dot_nt(left, right):
    return lax.dot_general(left, right, (((1,), (1,)), ((), ())), preferred_element_type=F32)


def place(index):
    return divmod(index * 4, 128)


def sends_kernel(f_hbm, a_hbm, w_hbm, fields, w_ref, xf, xl, yf, yl, zs, sems):
    copies = [
        pltpu.make_async_copy(f_hbm, fields.at[0:3], sems.at[0]),
        pltpu.make_async_copy(a_hbm, fields.at[3:6], sems.at[1]),
        pltpu.make_async_copy(w_hbm, w_ref, sems.at[2]),
    ]
    for copy in copies:
        copy.start()
    for copy in copies:
        copy.wait()
    comps, planes, rows = fields.shape[:3]
    xf[...] = fields[:, 0:2]
    xl[...] = fields[:, planes - 2 : planes]
    yf[...] = fields[:, :, 0:2, :]
    yl[...] = fields[:, :, rows - 2 : rows, :]
    lane = iota((8, 128), 1)
    packed = [jnp.zeros((8, 128), F32) for _ in range(zs.shape[0] // 8)]
    for comp in range(comps):
        for plane in range(planes):
            for half in range(rows // 8):
                group, at = place((comp * planes + plane) * (rows // 8) + half)
                tile = fields[comp, plane, 8 * half : 8 * half + 8, :]
                moved = pltpu.roll(tile, (2 + at) % 128, 1)
                here = (lane >= at) & (lane < at + 4)
                packed[group] = jnp.where(here, moved, packed[group])
    for group, tile in enumerate(packed):
        zs[8 * group : 8 * group + 8, :] = tile


def weights_kernel(w_ref, wk_ref):
    pairs = w_ref.shape[1]
    high, low = split(w_ref[...] * (1.0 / 144.0))
    q = iota((pairs, DEPTH), 1)
    p = iota((pairs, DEPTH), 0)
    r = jnp.where(q >= 2 * GROUP, q - 2 * GROUP, jnp.where(q >= GROUP, q - GROUP, q))
    wanted = jnp.where(r < 72, 9 * lax.shift_right_logical(r, 3) + (r & 7), 9 * (r - 72) + 8)
    wanted = jnp.where(q >= 3 * GROUP, pairs - 1, wanted)
    use_low = ((q >= 2 * GROUP) & (q < 3 * GROUP)) | (q == 3 * GROUP + 2)
    hit = (wanted == p) & (q < 3 * GROUP + 3)
    to_high = jnp.where(hit & ~use_low, 1.0, 0.0).astype(BF16)
    to_low = jnp.where(hit & use_low, 1.0, 0.0).astype(BF16)
    wk_ref[...] = (dot(high, to_high) + dot(low, to_low)).astype(BF16)


def compute_kernel(fields, xb, xa, yb, ya, zb, za, wk_ref, sh_ref, sl_ref, g_ref, ypad, grads):
    planes, rows = fields.shape[1], fields.shape[2]
    halves = rows // 8
    lane = iota((8, 128), 1)
    total = None
    ypad[:, :, 8 : 8 + rows, :] = fields[...]
    ypad[:, :, 6:8, :] = yb[...]
    ypad[:, :, 8 + rows : 10 + rows, :] = ya[...]

    def line(comp, plane):
        if plane < 0:
            return xb[comp, plane + 2]
        if plane >= planes:
            return xa[comp, plane - planes]
        return fields[comp, plane]

    def depth_slope(comp, plane, half):
        tile = fields[comp, plane, 8 * half : 8 * half + 8, :]
        group, at = place((comp * planes + plane) * halves + half)
        before = zb[8 * group : 8 * group + 8, :]
        after = za[8 * group : 8 * group + 8, :]
        up1 = jnp.where(lane < 1, pltpu.roll(before, (127 - at) % 128, 1), pltpu.roll(tile, 1, 1))
        up2 = jnp.where(lane < 2, pltpu.roll(before, (128 - at) % 128, 1), pltpu.roll(tile, 2, 1))
        dn1 = jnp.where(lane >= 127, pltpu.roll(after, (125 - at) % 128, 1), pltpu.roll(tile, 127, 1))
        dn2 = jnp.where(lane >= 126, pltpu.roll(after, (124 - at) % 128, 1), pltpu.roll(tile, 126, 1))
        return 8.0 * (dn1 - up1) - (dn2 - up2)

    lines = planes * rows
    third = iota((16, 128), 0)
    for plane in range(planes):
        for comp in range(6):
            dx = 8.0 * (line(comp, plane + 1) - line(comp, plane - 1)) - (
                line(comp, plane + 2) - line(comp, plane - 2)
            )
            y = lambda k: ypad[comp, plane, 8 + k : 8 + k + rows, :]
            dy = 8.0 * (y(1) - y(-1)) - (y(2) - y(-2))
            dz = jnp.concatenate([depth_slope(comp, plane, h) for h in range(halves)], 0)
            for dim, slope in enumerate((dx, dy, dz)):
                at = (3 * comp + dim) * lines + plane * rows
                grads[at : at + rows, :] = slope
        for first in range(plane * rows, (plane + 1) * rows, 2):
            columns = []
            for at in (first, first + 1):
                one = lambda entry: grads[entry * lines + at : entry * lines + at + 1, :]
                forward = grads[pl.ds(at, 8, stride=lines), :]
                adjoint = grads[pl.ds(9 * lines + at, 8, stride=lines), :]
                products = [one(a) * adjoint for a in range(9)] + [forward * one(17)]
                high, low = split(jnp.concatenate(products, 0))
                final = jnp.broadcast_to(one(8) * one(17), third.shape)
                final_high = final.astype(BF16).astype(F32)
                final = jnp.where(third == 1, final - final_high, final_high)
                final = jnp.where(third < 3, final, 0.0).astype(BF16)
                columns.append(jnp.concatenate([high, low, high, final], 0))
            block = dot(wk_ref[...], jnp.concatenate(columns, 1))
            high, low = split(block)
            sh_ref[:, 128 * first : 128 * first + 256] = high
            sl_ref[:, 128 * first : 128 * first + 256] = low
            both = jnp.concatenate([high, low], 0)
            part = dot_nt(both, jnp.concatenate([both, both], 0))
            total = part if total is None else total + part

    snaps = total.shape[0] // 2
    gram = total[:snaps] + total[snaps:]
    gram = gram + pltpu.roll(gram, snaps, 1)
    packed = gram[0:8]
    for k in range(1, snaps // 8):
        packed = jnp.where(lane >= 32 * k, gram[8 * k : 8 * k + 8], packed)
    g_ref[...] = jnp.broadcast_to(packed[None], g_ref.shape)


def inverse_factor(gram, snaps):
    row, lane = iota(gram.shape, 0), iota(gram.shape, 1)
    work = jnp.where(lane < snaps, gram, jnp.where(lane == row + snaps, 1.0, 0.0))
    for first in range(0, snaps, BLOCK):
        block = range(first, first + BLOCK)
        cols = [jnp.broadcast_to(work[:, k : k + 1], work.shape) for k in block]
        rows = [work[k : k + 1, :] for k in block]
        for i, k in enumerate(block):
            inverse = 1.0 / cols[i][k : k + 1, :]
            below = jnp.where(row > k, cols[i], 0.0)
            scaled = rows[i] * inverse
            work = work - below * scaled
            for j in range(i + 1, BLOCK):
                entry = cols[i][first + j : first + j + 1, :]
                cols[j] = cols[j] - below * (entry * inverse)
                rows[j] = rows[j] - entry * scaled
    diagonal = jnp.sum(jnp.where(lane == row, work, 0.0), axis=1, keepdims=True)
    work = work * (1.0 / jnp.sqrt(diagonal))
    return jnp.where(lane < snaps, pltpu.roll(work, 128 - snaps, 1), 0.0)


def basis_kernel(cells, r_ref, sh_ref, sl_ref, o_hbm, out_ref, sems):
    planes, snaps, rows, cols = out_ref.shape
    packed = r_ref[0]
    for i in range(1, r_ref.shape[0]):
        packed = packed + r_ref[i]
    packed = packed * (1.0 / cells)
    gram = jnp.concatenate(
        [packed] + [pltpu.roll(packed, 128 - 32 * k, 1) for k in range(1, snaps // 8)], 0
    )
    inverse = inverse_factor(gram, snaps)
    high = inverse.astype(BF16).astype(F32)
    low = inverse - high
    factor = high + pltpu.roll(high, snaps, 1)
    factor = factor + pltpu.roll(low, 2 * snaps, 1) + pltpu.roll(low, 3 * snaps, 1)
    factor = factor.astype(BF16)

    copies = []
    for plane in range(planes):
        part = slice(plane * rows * cols, (plane + 1) * rows * cols)
        both = jnp.concatenate([sh_ref[:, part], sl_ref[:, part]], 0)
        out = dot(factor, jnp.concatenate([both, both], 0))
        for y in range(rows):
            out_ref[plane, :, y, :] = out[:, cols * y : cols * y + cols]
        copy = pltpu.make_async_copy(out_ref.at[plane], o_hbm.at[:, plane], sems.at[plane])
        copy.start()
        copies.append(copy)
    for copy in copies:
        copy.wait()


def shape(*dims, dtype=F32):
    return jax.ShapeDtypeStruct(dims, dtype)


def body(forward_velocity, adjoint_velocity, weights):
    _, planes, rows, cols = forward_velocity.shape
    snaps = weights.shape[0]
    cells = planes * rows * cols
    zrows = -(-6 * planes * (rows // 8) * 4 // 128) * 8
    params = pltpu.CompilerParams(vmem_limit_bytes=48 * 2**20)

    fields, w, xf, xl, yf, yl, zs = pl.pallas_call(
        sends_kernel,
        in_specs=[HBM] * 3,
        out_specs=[VMEM] * 7,
        out_shape=[
            shape(6, planes, rows, cols),
            shape(*weights.shape),
            shape(6, 2, rows, cols),
            shape(6, 2, rows, cols),
            shape(6, planes, 2, cols),
            shape(6, planes, 2, cols),
            shape(zrows, 128),
        ],
        scratch_shapes=[pltpu.SemaphoreType.DMA((3,))],
        compiler_params=params,
        interpret=INTERPRET,
    )(*(pltpu.with_memory_space_constraint(x, pltpu.HBM) for x in (forward_velocity, adjoint_velocity, weights)))

    def move(value, axis, step):
        size = lax.axis_size(axis)
        return lax.ppermute(value, axis, [(i, (i + step) % size) for i in range(size)])

    xb, xa = move(xl, "stream", 1), move(xf, "stream", -1)
    yb, ya = move(yl, "span", 1), move(yf, "span", -1)
    zb = move(lax.optimization_barrier((zs, xb))[0], "depth", 1)
    za = move(lax.optimization_barrier((zs, xa))[0], "depth", -1)

    wk = pl.pallas_call(
        weights_kernel,
        in_specs=[VMEM],
        out_specs=VMEM,
        out_shape=shape(snaps, DEPTH, dtype=BF16),
        compiler_params=params,
        interpret=INTERPRET,
    )(w)

    span = lax.axis_size("span")
    others = lax.axis_size(("stream", "depth"))
    sh, sl, grams = pl.pallas_call(
        compute_kernel,
        in_specs=[VMEM] * 8,
        out_specs=[VMEM] * 3,
        out_shape=[
            shape(snaps, cells, dtype=BF16),
            shape(snaps, cells, dtype=BF16),
            shape(span, 8, 128),
        ],
        scratch_shapes=[
            pltpu.VMEM((6, planes, rows + 16, cols), F32),
            pltpu.VMEM((18 * planes * rows, cols), F32),
        ],
        compiler_params=params,
        interpret=INTERPRET,
    )(fields, xb, xa, yb, ya, zb, za, wk)

    grams = lax.all_to_all(grams, "span", 0, 0, tiled=True)
    grams = jnp.broadcast_to(grams.sum(0)[None], (others, 8, 128))
    grams = lax.all_to_all(grams, ("stream", "depth"), 0, 0, tiled=True)

    return pl.pallas_call(
        functools.partial(basis_kernel, cells * span * others),
        in_specs=[VMEM] * 3,
        out_specs=HBM,
        out_shape=shape(snaps, planes, rows, cols),
        scratch_shapes=[
            pltpu.VMEM((planes, snaps, rows, cols), F32),
            pltpu.SemaphoreType.DMA((planes,)),
        ],
        compiler_params=params,
        interpret=INTERPRET,
    )(grams, sh, sl)


def solution(mesh):
    spec = P(None, "stream", "span", "depth")
    return jax.shard_map(body, mesh=mesh, in_specs=(spec, spec, P()), out_specs=spec, check_vma=False)
```

```python
import functools

import jax
import jax.numpy as jnp
from jax import lax
from jax.experimental import pallas as pl
from jax.experimental.pallas import tpu as pltpu
from jax.sharding import PartitionSpec as P

F32 = jnp.float32
BF16 = jnp.bfloat16
INTERPRET = False
VMEM = pl.BlockSpec(memory_space=pltpu.VMEM)
HBM = pl.BlockSpec(memory_space=pltpu.HBM)
GROUP = 80
DEPTH = 256
BLOCK = 8


def iota(shape, dim):
    return lax.broadcasted_iota(jnp.int32, shape, dim)


def split(value):
    high = value.astype(BF16)
    low = (value - high.astype(F32)).astype(BF16)
    return high, low


def dot(left, right):
    return jnp.dot(left, right, preferred_element_type=F32)


def dot_nt(left, right):
    return lax.dot_general(left, right, (((1,), (1,)), ((), ())), preferred_element_type=F32)


def place(index):
    return divmod(index * 4, 128)


def sends_kernel(f_hbm, a_hbm, w_hbm, fields, w_ref, xf, xl, yf, yl, zs, sems):
    copies = [
        pltpu.make_async_copy(f_hbm, fields.at[0:3], sems.at[0]),
        pltpu.make_async_copy(a_hbm, fields.at[3:6], sems.at[1]),
        pltpu.make_async_copy(w_hbm, w_ref, sems.at[2]),
    ]
    for copy in copies:
        copy.start()
    for copy in copies:
        copy.wait()
    comps, planes, rows = fields.shape[:3]
    xf[...] = fields[:, 0:2]
    xl[...] = fields[:, planes - 2 : planes]
    yf[...] = fields[:, :, 0:2, :]
    yl[...] = fields[:, :, rows - 2 : rows, :]
    lane = iota((8, 128), 1)
    packed = [jnp.zeros((8, 128), F32) for _ in range(zs.shape[0] // 8)]
    for comp in range(comps):
        for plane in range(planes):
            for half in range(rows // 8):
                group, at = place((comp * planes + plane) * (rows // 8) + half)
                tile = fields[comp, plane, 8 * half : 8 * half + 8, :]
                moved = pltpu.roll(tile, (2 + at) % 128, 1)
                here = (lane >= at) & (lane < at + 4)
                packed[group] = jnp.where(here, moved, packed[group])
    for group, tile in enumerate(packed):
        zs[8 * group : 8 * group + 8, :] = tile


def weights_kernel(w_ref, wk_ref):
    pairs = w_ref.shape[1]
    high, low = split(w_ref[...] * (1.0 / 144.0))
    q = iota((pairs, DEPTH), 1)
    p = iota((pairs, DEPTH), 0)
    r = jnp.where(q >= 2 * GROUP, q - 2 * GROUP, jnp.where(q >= GROUP, q - GROUP, q))
    wanted = jnp.where(r < 72, 9 * lax.shift_right_logical(r, 3) + (r & 7), 9 * (r - 72) + 8)
    wanted = jnp.where(q >= 3 * GROUP, pairs - 1, wanted)
    use_low = ((q >= 2 * GROUP) & (q < 3 * GROUP)) | (q == 3 * GROUP + 2)
    hit = (wanted == p) & (q < 3 * GROUP + 3)
    to_high = jnp.where(hit & ~use_low, 1.0, 0.0).astype(BF16)
    to_low = jnp.where(hit & use_low, 1.0, 0.0).astype(BF16)
    wk_ref[...] = (dot(high, to_high) + dot(low, to_low)).astype(BF16)


def compute_kernel(fields, xb, xa, yb, ya, zb, za, wk_ref, sh_ref, sl_ref, g_ref, ypad, grads):
    planes, rows = fields.shape[1], fields.shape[2]
    halves = rows // 8
    lane = iota((8, 128), 1)
    total = None
    ypad[:, :, 8 : 8 + rows, :] = fields[...]
    ypad[:, :, 6:8, :] = yb[...]
    ypad[:, :, 8 + rows : 10 + rows, :] = ya[...]

    def line(comp, plane):
        if plane < 0:
            return xb[comp, plane + 2]
        if plane >= planes:
            return xa[comp, plane - planes]
        return fields[comp, plane]

    def depth_slope(comp, plane, half):
        tile = fields[comp, plane, 8 * half : 8 * half + 8, :]
        group, at = place((comp * planes + plane) * halves + half)
        before = zb[8 * group : 8 * group + 8, :]
        after = za[8 * group : 8 * group + 8, :]
        up1 = jnp.where(lane < 1, pltpu.roll(before, (127 - at) % 128, 1), pltpu.roll(tile, 1, 1))
        up2 = jnp.where(lane < 2, pltpu.roll(before, (128 - at) % 128, 1), pltpu.roll(tile, 2, 1))
        dn1 = jnp.where(lane >= 127, pltpu.roll(after, (125 - at) % 128, 1), pltpu.roll(tile, 127, 1))
        dn2 = jnp.where(lane >= 126, pltpu.roll(after, (124 - at) % 128, 1), pltpu.roll(tile, 126, 1))
        return 8.0 * (dn1 - up1) - (dn2 - up2)

    lines = planes * rows
    third = iota((16, 128), 0)
    for plane in range(planes):
        for comp in range(6):
            dx = 8.0 * (line(comp, plane + 1) - line(comp, plane - 1)) - (
                line(comp, plane + 2) - line(comp, plane - 2)
            )
            y = lambda k: ypad[comp, plane, 8 + k : 8 + k + rows, :]
            dy = 8.0 * (y(1) - y(-1)) - (y(2) - y(-2))
            dz = jnp.concatenate([depth_slope(comp, plane, h) for h in range(halves)], 0)
            for dim, slope in enumerate((dx, dy, dz)):
                at = (3 * comp + dim) * lines + plane * rows
                grads[at : at + rows, :] = slope
        for first in range(plane * rows, (plane + 1) * rows, 2):
            columns = []
            for at in (first, first + 1):
                one = lambda entry: grads[entry * lines + at : entry * lines + at + 1, :]
                forward = grads[pl.ds(at, 8, stride=lines), :]
                adjoint = grads[pl.ds(9 * lines + at, 8, stride=lines), :]
                products = [one(a) * adjoint for a in range(9)] + [forward * one(17)]
                high, low = split(jnp.concatenate(products, 0))
                final = jnp.broadcast_to(one(8) * one(17), third.shape)
                final_high = final.astype(BF16).astype(F32)
                final = jnp.where(third == 1, final - final_high, final_high)
                final = jnp.where(third < 3, final, 0.0).astype(BF16)
                columns.append(jnp.concatenate([high, low, high, final], 0))
            block = dot(wk_ref[...], jnp.concatenate(columns, 1))
            high, low = split(block)
            sh_ref[:, 128 * first : 128 * first + 256] = high
            sl_ref[:, 128 * first : 128 * first + 256] = low
            both = jnp.concatenate([high, low], 0)
            part = dot_nt(both, jnp.concatenate([both, both], 0))
            total = part if total is None else total + part

    snaps = total.shape[0] // 2
    gram = total[:snaps] + total[snaps:]
    gram = gram + pltpu.roll(gram, snaps, 1)
    packed = gram[0:8]
    for k in range(1, snaps // 8):
        packed = jnp.where(lane >= 32 * k, gram[8 * k : 8 * k + 8], packed)
    g_ref[...] = jnp.broadcast_to(packed[None], g_ref.shape)


def inverse_factor(gram, snaps):
    row, lane = iota(gram.shape, 0), iota(gram.shape, 1)
    work = jnp.where(lane < snaps, gram, jnp.where(lane == row + snaps, 1.0, 0.0))
    for first in range(0, snaps, BLOCK):
        block = range(first, first + BLOCK)
        cols = [jnp.broadcast_to(work[:, k : k + 1], work.shape) for k in block]
        rows = [work[k : k + 1, :] for k in block]
        for i, k in enumerate(block):
            inverse = 1.0 / cols[i][k : k + 1, :]
            below = jnp.where(row > k, cols[i], 0.0)
            scaled = rows[i] * inverse
            work = work - below * scaled
            for j in range(i + 1, BLOCK):
                entry = cols[i][first + j : first + j + 1, :]
                cols[j] = cols[j] - below * (entry * inverse)
                rows[j] = rows[j] - entry * scaled
    diagonal = jnp.sum(jnp.where(lane == row, work, 0.0), axis=1, keepdims=True)
    work = work * (1.0 / jnp.sqrt(diagonal))
    return jnp.where(lane < snaps, pltpu.roll(work, 128 - snaps, 1), 0.0)


def basis_kernel(cells, r_ref, sh_ref, sl_ref, o_hbm, out_ref, sems):
    planes, snaps, rows, cols = out_ref.shape
    packed = r_ref[0]
    for i in range(1, r_ref.shape[0]):
        packed = packed + r_ref[i]
    packed = packed * (1.0 / cells)
    gram = jnp.concatenate(
        [packed] + [pltpu.roll(packed, 128 - 32 * k, 1) for k in range(1, snaps // 8)], 0
    )
    inverse = inverse_factor(gram, snaps)
    high = inverse.astype(BF16).astype(F32)
    low = inverse - high
    factor = high + pltpu.roll(high, snaps, 1)
    factor = factor + pltpu.roll(low, 2 * snaps, 1) + pltpu.roll(low, 3 * snaps, 1)
    factor = factor.astype(BF16)

    flat = out_ref.reshape(planes * snaps * rows, cols)
    copies = []
    for plane in range(planes):
        part = slice(plane * rows * cols, (plane + 1) * rows * cols)
        both = jnp.concatenate([sh_ref[:, part], sl_ref[:, part]], 0)
        out = dot(factor, jnp.concatenate([both, both], 0))
        for y in range(rows):
            flat[pl.ds(plane * snaps * rows + y, snaps, stride=rows), :] = out[:, cols * y : cols * y + cols]
        copy = pltpu.make_async_copy(out_ref.at[plane], o_hbm.at[:, plane], sems.at[plane])
        copy.start()
        copies.append(copy)
    for copy in copies:
        copy.wait()


def shape(*dims, dtype=F32):
    return jax.ShapeDtypeStruct(dims, dtype)


def body(forward_velocity, adjoint_velocity, weights):
    _, planes, rows, cols = forward_velocity.shape
    snaps = weights.shape[0]
    cells = planes * rows * cols
    zrows = -(-6 * planes * (rows // 8) * 4 // 128) * 8
    params = pltpu.CompilerParams(vmem_limit_bytes=48 * 2**20)

    fields, w, xf, xl, yf, yl, zs = pl.pallas_call(
        sends_kernel,
        in_specs=[HBM] * 3,
        out_specs=[VMEM] * 7,
        out_shape=[
            shape(6, planes, rows, cols),
            shape(*weights.shape),
            shape(6, 2, rows, cols),
            shape(6, 2, rows, cols),
            shape(6, planes, 2, cols),
            shape(6, planes, 2, cols),
            shape(zrows, 128),
        ],
        scratch_shapes=[pltpu.SemaphoreType.DMA((3,))],
        compiler_params=params,
        interpret=INTERPRET,
    )(*(pltpu.with_memory_space_constraint(x, pltpu.HBM) for x in (forward_velocity, adjoint_velocity, weights)))

    def move(value, axis, step):
        size = lax.axis_size(axis)
        return lax.ppermute(value, axis, [(i, (i + step) % size) for i in range(size)])

    xb, xa = move(xl, "stream", 1), move(xf, "stream", -1)
    yb, ya = move(yl, "span", 1), move(yf, "span", -1)
    zb = move(lax.optimization_barrier((zs, xb))[0], "depth", 1)
    za = move(lax.optimization_barrier((zs, xa))[0], "depth", -1)

    wk = pl.pallas_call(
        weights_kernel,
        in_specs=[VMEM],
        out_specs=VMEM,
        out_shape=shape(snaps, DEPTH, dtype=BF16),
        compiler_params=params,
        interpret=INTERPRET,
    )(w)

    span = lax.axis_size("span")
    others = lax.axis_size(("stream", "depth"))
    sh, sl, grams = pl.pallas_call(
        compute_kernel,
        in_specs=[VMEM] * 8,
        out_specs=[VMEM] * 3,
        out_shape=[
            shape(snaps, cells, dtype=BF16),
            shape(snaps, cells, dtype=BF16),
            shape(span, 8, 128),
        ],
        scratch_shapes=[
            pltpu.VMEM((6, planes, rows + 16, cols), F32),
            pltpu.VMEM((18 * planes * rows, cols), F32),
        ],
        compiler_params=params,
        interpret=INTERPRET,
    )(fields, xb, xa, yb, ya, zb, za, wk)

    grams = lax.all_to_all(grams, "span", 0, 0, tiled=True)
    grams = jnp.broadcast_to(grams.sum(0)[None], (others, 8, 128))
    grams = lax.all_to_all(grams, ("stream", "depth"), 0, 0, tiled=True)

    return pl.pallas_call(
        functools.partial(basis_kernel, cells * span * others),
        in_specs=[VMEM] * 3,
        out_specs=HBM,
        out_shape=shape(snaps, planes, rows, cols),
        scratch_shapes=[
            pltpu.VMEM((planes, snaps, rows, cols), F32),
            pltpu.SemaphoreType.DMA((planes,)),
        ],
        compiler_params=params,
        interpret=INTERPRET,
    )(grams, sh, sl)


def solution(mesh):
    spec = P(None, "stream", "span", "depth")
    return jax.shard_map(body, mesh=mesh, in_specs=(spec, spec, P()), out_specs=spec, check_vma=False)
```

```python
import functools

import jax
import jax.numpy as jnp
from jax import lax
from jax.experimental import pallas as pl
from jax.experimental.pallas import tpu as pltpu
from jax.sharding import PartitionSpec as P

F32 = jnp.float32
BF16 = jnp.bfloat16
INTERPRET = False
VMEM = pl.BlockSpec(memory_space=pltpu.VMEM)
HBM = pl.BlockSpec(memory_space=pltpu.HBM)
GROUP = 80
DEPTH = 256
BLOCK = 8


def iota(shape, dim):
    return lax.broadcasted_iota(jnp.int32, shape, dim)


def split(value):
    high = value.astype(BF16)
    low = (value - high.astype(F32)).astype(BF16)
    return high, low


def dot(left, right):
    return jnp.dot(left, right, preferred_element_type=F32)


def dot_nt(left, right):
    return lax.dot_general(left, right, (((1,), (1,)), ((), ())), preferred_element_type=F32)


def place(index):
    return divmod(index * 4, 128)


def sends_kernel(f_hbm, a_hbm, w_hbm, fields, w_ref, xf, xl, yf, yl, zs, sems):
    copies = [
        pltpu.make_async_copy(f_hbm, fields.at[0:3], sems.at[0]),
        pltpu.make_async_copy(a_hbm, fields.at[3:6], sems.at[1]),
        pltpu.make_async_copy(w_hbm, w_ref, sems.at[2]),
    ]
    for copy in copies:
        copy.start()
    for copy in copies:
        copy.wait()
    comps, planes, rows = fields.shape[:3]
    xf[...] = fields[:, 0:2]
    xl[...] = fields[:, planes - 2 : planes]
    yf[...] = fields[:, :, 0:2, :]
    yl[...] = fields[:, :, rows - 2 : rows, :]
    lane = iota((8, 128), 1)
    packed = [jnp.zeros((8, 128), F32) for _ in range(zs.shape[0] // 8)]
    for comp in range(comps):
        for plane in range(planes):
            for half in range(rows // 8):
                group, at = place((comp * planes + plane) * (rows // 8) + half)
                tile = fields[comp, plane, 8 * half : 8 * half + 8, :]
                moved = pltpu.roll(tile, (2 + at) % 128, 1)
                here = (lane >= at) & (lane < at + 4)
                packed[group] = jnp.where(here, moved, packed[group])
    for group, tile in enumerate(packed):
        zs[8 * group : 8 * group + 8, :] = tile


def weights_kernel(w_ref, wk_ref):
    pairs = w_ref.shape[1]
    high, low = split(w_ref[...] * (1.0 / 144.0))
    q = iota((pairs, DEPTH), 1)
    p = iota((pairs, DEPTH), 0)
    r = jnp.where(q >= 2 * GROUP, q - 2 * GROUP, jnp.where(q >= GROUP, q - GROUP, q))
    wanted = jnp.where(r < 72, 9 * lax.shift_right_logical(r, 3) + (r & 7), 9 * (r - 72) + 8)
    wanted = jnp.where(q >= 3 * GROUP, pairs - 1, wanted)
    use_low = ((q >= 2 * GROUP) & (q < 3 * GROUP)) | (q == 3 * GROUP + 2)
    hit = (wanted == p) & (q < 3 * GROUP + 3)
    to_high = jnp.where(hit & ~use_low, 1.0, 0.0).astype(BF16)
    to_low = jnp.where(hit & use_low, 1.0, 0.0).astype(BF16)
    wk_ref[...] = (dot(high, to_high) + dot(low, to_low)).astype(BF16)


def compute_kernel(fields, xb, xa, yb, ya, zb, za, wk_ref, sh_ref, sl_ref, g_ref, ypad, grads):
    planes, rows = fields.shape[1], fields.shape[2]
    halves = rows // 8
    lane = iota((8, 128), 1)
    total = None
    ypad[:, :, 8 : 8 + rows, :] = fields[...]
    ypad[:, :, 6:8, :] = yb[...]
    ypad[:, :, 8 + rows : 10 + rows, :] = ya[...]

    def line(comp, plane):
        if plane < 0:
            return xb[comp, plane + 2]
        if plane >= planes:
            return xa[comp, plane - planes]
        return fields[comp, plane]

    def depth_slope(comp, plane, half):
        tile = fields[comp, plane, 8 * half : 8 * half + 8, :]
        group, at = place((comp * planes + plane) * halves + half)
        before = zb[8 * group : 8 * group + 8, :]
        after = za[8 * group : 8 * group + 8, :]
        up1 = jnp.where(lane < 1, pltpu.roll(before, (127 - at) % 128, 1), pltpu.roll(tile, 1, 1))
        up2 = jnp.where(lane < 2, pltpu.roll(before, (128 - at) % 128, 1), pltpu.roll(tile, 2, 1))
        dn1 = jnp.where(lane >= 127, pltpu.roll(after, (125 - at) % 128, 1), pltpu.roll(tile, 127, 1))
        dn2 = jnp.where(lane >= 126, pltpu.roll(after, (124 - at) % 128, 1), pltpu.roll(tile, 126, 1))
        return 8.0 * (dn1 - up1) - (dn2 - up2)

    lines = planes * rows
    third = iota((16, 128), 0)
    for plane in range(planes):
        for comp in range(6):
            dx = 8.0 * (line(comp, plane + 1) - line(comp, plane - 1)) - (
                line(comp, plane + 2) - line(comp, plane - 2)
            )
            y = lambda k: ypad[comp, plane, 8 + k : 8 + k + rows, :]
            dy = 8.0 * (y(1) - y(-1)) - (y(2) - y(-2))
            dz = jnp.concatenate([depth_slope(comp, plane, h) for h in range(halves)], 0)
            for dim, slope in enumerate((dx, dy, dz)):
                at = (3 * comp + dim) * lines + plane * rows
                grads[at : at + rows, :] = slope
        for first in range(plane * rows, (plane + 1) * rows, 2):
            columns = []
            for at in (first, first + 1):
                one = lambda entry: grads[entry * lines + at : entry * lines + at + 1, :]
                forward = grads[pl.ds(at, 8, stride=lines), :]
                adjoint = grads[pl.ds(9 * lines + at, 8, stride=lines), :]
                products = [one(a) * adjoint for a in range(9)] + [forward * one(17)]
                high, low = split(jnp.concatenate(products, 0))
                final = jnp.broadcast_to(one(8) * one(17), third.shape)
                final_high = final.astype(BF16).astype(F32)
                final = jnp.where(third == 1, final - final_high, final_high)
                final = jnp.where(third < 3, final, 0.0).astype(BF16)
                columns.append(jnp.concatenate([high, low, high, final], 0))
            block = dot(wk_ref[...], jnp.concatenate(columns, 1))
            high, low = split(block)
            sh_ref[:, 128 * first : 128 * first + 256] = high
            sl_ref[:, 128 * first : 128 * first + 256] = low
            both = jnp.concatenate([high, low], 0)
            part = dot_nt(both, jnp.concatenate([both, both], 0))
            total = part if total is None else total + part

    snaps = total.shape[0] // 2
    gram = total[:snaps] + total[snaps:]
    gram = gram + pltpu.roll(gram, snaps, 1)
    row, wide = iota((16, 128), 0), iota((16, 128), 1)
    half = jnp.where(((wide - row) & 31) < 16, gram[0:16], gram[16:32])
    middle = jnp.sum(jnp.where((wide & 31) == row + 16, gram[0:16], 0.0), axis=0, keepdims=True)
    parts = [half[0:8], pltpu.roll(half[0:8], 4, 0), half[8:16], pltpu.roll(half[8:16], 4, 0)]
    packed = parts[0]
    for k in range(1, 4):
        packed = jnp.where(lane >= 32 * k, parts[k], packed)
    for j in range(5):
        line = packed[j : j + 1] if j < 4 else middle
        g_ref[:, :, 128 * j : 128 * j + 128] = jnp.broadcast_to(line[None], (g_ref.shape[0], 1, 128))


def inverse_factor(gram, snaps):
    row, lane = iota(gram.shape, 0), iota(gram.shape, 1)
    work = jnp.where(lane < snaps, gram, jnp.where(lane == row + snaps, 1.0, 0.0))
    for first in range(0, snaps, BLOCK):
        block = range(first, first + BLOCK)
        cols = [jnp.broadcast_to(work[:, k : k + 1], work.shape) for k in block]
        rows = [work[k : k + 1, :] for k in block]
        for i, k in enumerate(block):
            inverse = 1.0 / cols[i][k : k + 1, :]
            below = jnp.where(row > k, cols[i], 0.0)
            scaled = rows[i] * inverse
            work = work - below * scaled
            for j in range(i + 1, BLOCK):
                entry = cols[i][first + j : first + j + 1, :]
                cols[j] = cols[j] - below * (entry * inverse)
                rows[j] = rows[j] - entry * scaled
    diagonal = jnp.sum(jnp.where(lane == row, work, 0.0), axis=1, keepdims=True)
    work = work * (1.0 / jnp.sqrt(diagonal))
    return jnp.where(lane < snaps, pltpu.roll(work, 128 - snaps, 1), 0.0)


def basis_kernel(cells, r_ref, sh_ref, sl_ref, o_hbm, out_ref, sems):
    planes, snaps, rows, cols = out_ref.shape
    packed = r_ref[0]
    for i in range(1, r_ref.shape[0]):
        packed = packed + r_ref[i]
    packed = packed * (1.0 / cells)
    row8 = iota((8, 128), 0)
    quad = jnp.zeros((8, 128), F32)
    for j in range(4):
        quad = jnp.where((row8 & 3) == j, packed[:, 128 * j : 128 * j + 128], quad)
    turned = [quad] + [pltpu.roll(quad, 128 - 32 * k, 1) for k in range(1, 4)]
    half = [jnp.where(row8 < 4, turned[2 * k], turned[2 * k + 1]) for k in range(2)]
    half = jnp.concatenate(half + half, 0)
    row, wide = iota((snaps, 128), 0), iota((snaps, 128), 1)
    middle = (row < 16) & (wide == row + 16)
    half = jnp.where(middle, packed[:, 512:640], half)
    known = (wide < snaps) & (middle | (((wide - row) & 31) < 16))
    half = jnp.where(known, half, 0.0)
    mirror = jnp.concatenate([half, jnp.zeros((128 - snaps, 128), F32)], 0).T[0:snaps]
    gram = jnp.where(known, half, mirror)
    inverse = inverse_factor(gram, snaps)
    high = inverse.astype(BF16).astype(F32)
    low = inverse - high
    factor = high + pltpu.roll(high, snaps, 1)
    factor = factor + pltpu.roll(low, 2 * snaps, 1) + pltpu.roll(low, 3 * snaps, 1)
    factor = factor.astype(BF16)

    flat = out_ref.reshape(planes * snaps * rows, cols)
    copies = []
    for plane in range(planes):
        part = slice(plane * rows * cols, (plane + 1) * rows * cols)
        both = jnp.concatenate([sh_ref[:, part], sl_ref[:, part]], 0)
        out = dot(factor, jnp.concatenate([both, both], 0))
        for y in range(rows):
            flat[pl.ds(plane * snaps * rows + y, snaps, stride=rows), :] = out[:, cols * y : cols * y + cols]
        copy = pltpu.make_async_copy(out_ref.at[plane], o_hbm.at[:, plane], sems.at[plane])
        copy.start()
        copies.append(copy)
    for copy in copies:
        copy.wait()


def shape(*dims, dtype=F32):
    return jax.ShapeDtypeStruct(dims, dtype)


def body(forward_velocity, adjoint_velocity, weights):
    _, planes, rows, cols = forward_velocity.shape
    snaps = weights.shape[0]
    cells = planes * rows * cols
    zrows = -(-6 * planes * (rows // 8) * 4 // 128) * 8
    params = pltpu.CompilerParams(vmem_limit_bytes=48 * 2**20)

    fields, w, xf, xl, yf, yl, zs = pl.pallas_call(
        sends_kernel,
        in_specs=[HBM] * 3,
        out_specs=[VMEM] * 7,
        out_shape=[
            shape(6, planes, rows, cols),
            shape(*weights.shape),
            shape(6, 2, rows, cols),
            shape(6, 2, rows, cols),
            shape(6, planes, 2, cols),
            shape(6, planes, 2, cols),
            shape(zrows, 128),
        ],
        scratch_shapes=[pltpu.SemaphoreType.DMA((3,))],
        compiler_params=params,
        interpret=INTERPRET,
    )(*(pltpu.with_memory_space_constraint(x, pltpu.HBM) for x in (forward_velocity, adjoint_velocity, weights)))

    def move(value, axis, step):
        size = lax.axis_size(axis)
        return lax.ppermute(value, axis, [(i, (i + step) % size) for i in range(size)])

    xb, xa = move(xl, "stream", 1), move(xf, "stream", -1)
    yb, ya = move(yl, "span", 1), move(yf, "span", -1)
    zb = move(lax.optimization_barrier((zs, xb))[0], "depth", 1)
    za = move(lax.optimization_barrier((zs, xa))[0], "depth", -1)

    wk = pl.pallas_call(
        weights_kernel,
        in_specs=[VMEM],
        out_specs=VMEM,
        out_shape=shape(snaps, DEPTH, dtype=BF16),
        compiler_params=params,
        interpret=INTERPRET,
    )(w)

    span = lax.axis_size("span")
    others = lax.axis_size(("stream", "depth"))
    sh, sl, grams = pl.pallas_call(
        compute_kernel,
        in_specs=[VMEM] * 8,
        out_specs=[VMEM] * 3,
        out_shape=[
            shape(snaps, cells, dtype=BF16),
            shape(snaps, cells, dtype=BF16),
            shape(span, 1, 640),
        ],
        scratch_shapes=[
            pltpu.VMEM((6, planes, rows + 16, cols), F32),
            pltpu.VMEM((18 * planes * rows, cols), F32),
        ],
        compiler_params=params,
        interpret=INTERPRET,
    )(fields, xb, xa, yb, ya, zb, za, wk)

    grams = lax.all_to_all(grams, "span", 0, 0, tiled=True)
    grams = jnp.broadcast_to(grams.sum(0)[None], (others, 1, 640))
    grams = lax.all_to_all(grams, ("stream", "depth"), 0, 0, tiled=True)

    return pl.pallas_call(
        functools.partial(basis_kernel, cells * span * others),
        in_specs=[VMEM] * 3,
        out_specs=HBM,
        out_shape=shape(snaps, planes, rows, cols),
        scratch_shapes=[
            pltpu.VMEM((planes, snaps, rows, cols), F32),
            pltpu.SemaphoreType.DMA((planes,)),
        ],
        compiler_params=params,
        interpret=INTERPRET,
    )(grams, sh, sl)


def solution(mesh):
    spec = P(None, "stream", "span", "depth")
    return jax.shard_map(body, mesh=mesh, in_specs=(spec, spec, P()), out_specs=spec, check_vma=False)
```

```python
import functools

import jax
import jax.numpy as jnp
from jax import lax
from jax.experimental import pallas as pl
from jax.experimental.pallas import tpu as pltpu
from jax.sharding import PartitionSpec as P

F32 = jnp.float32
BF16 = jnp.bfloat16
INTERPRET = False
VMEM = pl.BlockSpec(memory_space=pltpu.VMEM)
HBM = pl.BlockSpec(memory_space=pltpu.HBM)
GROUP = 80
DEPTH = 256
BLOCK = 8


def iota(shape, dim):
    return lax.broadcasted_iota(jnp.int32, shape, dim)


def split(value):
    high = value.astype(BF16)
    low = (value - high.astype(F32)).astype(BF16)
    return high, low


def dot(left, right):
    return jnp.dot(left, right, preferred_element_type=F32)


def dot_nt(left, right):
    return lax.dot_general(left, right, (((1,), (1,)), ((), ())), preferred_element_type=F32)


def place(index):
    return divmod(index * 4, 128)


def sends_kernel(f_hbm, a_hbm, w_hbm, fields, w_ref, xf, xl, yf, yl, zs, sems):
    copies = [
        pltpu.make_async_copy(f_hbm, fields.at[0:3], sems.at[0]),
        pltpu.make_async_copy(a_hbm, fields.at[3:6], sems.at[1]),
        pltpu.make_async_copy(w_hbm, w_ref, sems.at[2]),
    ]
    for copy in copies:
        copy.start()
    for copy in copies:
        copy.wait()
    comps, planes, rows = fields.shape[:3]
    xf[...] = fields[:, 0:2]
    xl[...] = fields[:, planes - 2 : planes]
    yf[...] = fields[:, :, 0:2, :]
    yl[...] = fields[:, :, rows - 2 : rows, :]
    lane = iota((8, 128), 1)
    packed = [jnp.zeros((8, 128), F32) for _ in range(zs.shape[0] // 8)]
    for comp in range(comps):
        for plane in range(planes):
            for half in range(rows // 8):
                group, at = place((comp * planes + plane) * (rows // 8) + half)
                tile = fields[comp, plane, 8 * half : 8 * half + 8, :]
                moved = pltpu.roll(tile, (2 + at) % 128, 1)
                here = (lane >= at) & (lane < at + 4)
                packed[group] = jnp.where(here, moved, packed[group])
    for group, tile in enumerate(packed):
        zs[8 * group : 8 * group + 8, :] = tile


def weights_kernel(w_ref, wk_ref):
    pairs = w_ref.shape[1]
    high, low = split(w_ref[...] * (1.0 / 144.0))
    q = iota((pairs, DEPTH), 1)
    p = iota((pairs, DEPTH), 0)
    r = jnp.where(q >= 2 * GROUP, q - 2 * GROUP, jnp.where(q >= GROUP, q - GROUP, q))
    wanted = jnp.where(r < 72, 9 * lax.shift_right_logical(r, 3) + (r & 7), 9 * (r - 72) + 8)
    wanted = jnp.where(q >= 3 * GROUP, pairs - 1, wanted)
    use_low = ((q >= 2 * GROUP) & (q < 3 * GROUP)) | (q == 3 * GROUP + 2)
    hit = (wanted == p) & (q < 3 * GROUP + 3)
    to_high = jnp.where(hit & ~use_low, 1.0, 0.0).astype(BF16)
    to_low = jnp.where(hit & use_low, 1.0, 0.0).astype(BF16)
    wk_ref[...] = (dot(high, to_high) + dot(low, to_low)).astype(BF16)


def compute_kernel(fields, xb, xa, yb, ya, zb, za, wk_ref, sh_ref, sl_ref, g_ref, ypad, grads):
    planes, rows = fields.shape[1], fields.shape[2]
    halves = rows // 8
    lane = iota((8, 128), 1)
    total = None
    ypad[:, :, 8 : 8 + rows, :] = fields[...]
    ypad[:, :, 6:8, :] = yb[...]
    ypad[:, :, 8 + rows : 10 + rows, :] = ya[...]

    def line(comp, plane):
        if plane < 0:
            return xb[comp, plane + 2]
        if plane >= planes:
            return xa[comp, plane - planes]
        return fields[comp, plane]

    def depth_slope(comp, plane, half):
        tile = fields[comp, plane, 8 * half : 8 * half + 8, :]
        group, at = place((comp * planes + plane) * halves + half)
        before = zb[8 * group : 8 * group + 8, :]
        after = za[8 * group : 8 * group + 8, :]
        up1 = jnp.where(lane < 1, pltpu.roll(before, (127 - at) % 128, 1), pltpu.roll(tile, 1, 1))
        up2 = jnp.where(lane < 2, pltpu.roll(before, (128 - at) % 128, 1), pltpu.roll(tile, 2, 1))
        dn1 = jnp.where(lane >= 127, pltpu.roll(after, (125 - at) % 128, 1), pltpu.roll(tile, 127, 1))
        dn2 = jnp.where(lane >= 126, pltpu.roll(after, (124 - at) % 128, 1), pltpu.roll(tile, 126, 1))
        return 8.0 * (dn1 - up1) - (dn2 - up2)

    lines = planes * rows
    third = iota((16, 128), 0)
    for plane in range(planes):
        for comp in range(6):
            dx = 8.0 * (line(comp, plane + 1) - line(comp, plane - 1)) - (
                line(comp, plane + 2) - line(comp, plane - 2)
            )
            y = lambda k: ypad[comp, plane, 8 + k : 8 + k + rows, :]
            dy = 8.0 * (y(1) - y(-1)) - (y(2) - y(-2))
            dz = jnp.concatenate([depth_slope(comp, plane, h) for h in range(halves)], 0)
            for dim, slope in enumerate((dx, dy, dz)):
                at = (3 * comp + dim) * lines + plane * rows
                grads[at : at + rows, :] = slope
        for first in range(plane * rows, (plane + 1) * rows, 2):
            columns = []
            for at in (first, first + 1):
                one = lambda entry: grads[entry * lines + at : entry * lines + at + 1, :]
                forward = grads[pl.ds(at, 8, stride=lines), :]
                adjoint = grads[pl.ds(9 * lines + at, 8, stride=lines), :]
                products = [one(a) * adjoint for a in range(9)] + [forward * one(17)]
                high, low = split(jnp.concatenate(products, 0))
                final = jnp.broadcast_to(one(8) * one(17), third.shape)
                final_high = final.astype(BF16).astype(F32)
                final = jnp.where(third == 1, final - final_high, final_high)
                final = jnp.where(third < 3, final, 0.0).astype(BF16)
                columns.append(jnp.concatenate([high, low, high, final], 0))
            block = dot(wk_ref[...], jnp.concatenate(columns, 1))
            high, low = split(block)
            sh_ref[:, 128 * first : 128 * first + 256] = high
            sl_ref[:, 128 * first : 128 * first + 256] = low
            both = jnp.concatenate([high, low], 0)
            part = dot_nt(both, jnp.concatenate([both, both], 0))
            total = part if total is None else total + part

    snaps = total.shape[0] // 2
    gram = total[:snaps] + total[snaps:]
    gram = gram + pltpu.roll(gram, snaps, 1)
    row, wide = iota((16, 128), 0), iota((16, 128), 1)
    half = jnp.where(((wide - row) & 31) < 16, gram[0:16], gram[16:32])
    middle = jnp.sum(jnp.where((wide & 31) == row + 16, gram[0:16], 0.0), axis=0, keepdims=True)
    parts = [half[0:8], pltpu.roll(half[0:8], 4, 0), half[8:16], pltpu.roll(half[8:16], 4, 0)]
    packed = parts[0]
    for k in range(1, 4):
        packed = jnp.where(lane >= 32 * k, parts[k], packed)
    for j in range(5):
        line = packed[j : j + 1] if j < 4 else middle
        g_ref[:, :, 128 * j : 128 * j + 128] = jnp.broadcast_to(line[None], (g_ref.shape[0], 1, 128))


def inverse_factor(gram, snaps):
    row, lane = iota(gram.shape, 0), iota(gram.shape, 1)
    work = jnp.where(lane < snaps, gram, jnp.where(lane == row + snaps, 1.0, 0.0))
    for first in range(0, snaps, BLOCK):
        block = range(first, first + BLOCK)
        cols = [jnp.broadcast_to(work[:, k : k + 1], work.shape) for k in block]
        rows = [work[k : k + 1, :] for k in block]
        for i, k in enumerate(block):
            inverse = 1.0 / cols[i][k : k + 1, :]
            below = jnp.where(row > k, cols[i], 0.0)
            scaled = rows[i] * inverse
            work = work - below * scaled
            for j in range(i + 1, BLOCK):
                entry = cols[i][first + j : first + j + 1, :]
                cols[j] = cols[j] - below * (entry * inverse)
                rows[j] = rows[j] - entry * scaled
    diagonal = jnp.sum(jnp.where(lane == row, work, 0.0), axis=1, keepdims=True)
    work = work * (1.0 / jnp.sqrt(diagonal))
    return jnp.where(lane < snaps, pltpu.roll(work, 128 - snaps, 1), 0.0)


def basis_kernel(cells, r_ref, sh_ref, sl_ref, o_hbm, out_ref, sems):
    planes, snaps, rows, cols = out_ref.shape
    packed = r_ref[0]
    for i in range(1, r_ref.shape[0]):
        packed = packed + r_ref[i]
    packed = packed * (1.0 / cells)
    row8 = iota((8, 128), 0)
    quad = jnp.zeros((8, 128), F32)
    for j in range(4):
        quad = jnp.where((row8 & 3) == j, packed[:, 128 * j : 128 * j + 128], quad)
    turned = [quad] + [pltpu.roll(quad, 128 - 32 * k, 1) for k in range(1, 4)]
    half = [jnp.where(row8 < 4, turned[2 * k], turned[2 * k + 1]) for k in range(2)]
    half = jnp.concatenate(half + half, 0)
    row, wide = iota((snaps, 128), 0), iota((snaps, 128), 1)
    middle = (row < 16) & (wide == row + 16)
    half = jnp.where(middle, packed[:, 512:640], half)
    known = (wide < snaps) & (middle | (((wide - row) & 31) < 16))
    half = jnp.where(known, half, 0.0)
    mirror = jnp.concatenate([half, jnp.zeros((128 - snaps, 128), F32)], 0).T[0:snaps]
    gram = jnp.where(known, half, mirror)
    inverse = inverse_factor(gram, snaps)
    high = inverse.astype(BF16).astype(F32)
    low = inverse - high
    factor = high + pltpu.roll(high, snaps, 1)
    factor = factor + pltpu.roll(low, 2 * snaps, 1) + pltpu.roll(low, 3 * snaps, 1)
    factor = factor.astype(BF16)

    flat = out_ref.reshape(planes * snaps * rows, cols)
    copies = []
    for plane in range(planes):
        part = slice(plane * rows * cols, (plane + 1) * rows * cols)
        both = jnp.concatenate([sh_ref[:, part], sl_ref[:, part]], 0)
        out = dot(factor, jnp.concatenate([both, both], 0))
        for y in range(rows):
            flat[pl.ds(plane * snaps * rows + y, snaps, stride=rows), :] = out[:, cols * y : cols * y + cols]
        copy = pltpu.make_async_copy(out_ref.at[plane], o_hbm.at[:, plane], sems.at[plane])
        copy.start()
        copies.append(copy)
    for copy in copies:
        copy.wait()


def shape(*dims, dtype=F32):
    return jax.ShapeDtypeStruct(dims, dtype)


def body(forward_velocity, adjoint_velocity, weights):
    _, planes, rows, cols = forward_velocity.shape
    snaps = weights.shape[0]
    cells = planes * rows * cols
    zrows = -(-6 * planes * (rows // 8) * 4 // 128) * 8
    params = pltpu.CompilerParams(vmem_limit_bytes=48 * 2**20)

    fields, w, xf, xl, yf, yl, zs = pl.pallas_call(
        sends_kernel,
        in_specs=[HBM] * 3,
        out_specs=[VMEM] * 7,
        out_shape=[
            shape(6, planes, rows, cols),
            shape(*weights.shape),
            shape(6, 2, rows, cols),
            shape(6, 2, rows, cols),
            shape(6, planes, 2, cols),
            shape(6, planes, 2, cols),
            shape(zrows, 128),
        ],
        scratch_shapes=[pltpu.SemaphoreType.DMA((3,))],
        compiler_params=params,
        interpret=INTERPRET,
    )(*(pltpu.with_memory_space_constraint(x, pltpu.HBM) for x in (forward_velocity, adjoint_velocity, weights)))

    def move(value, axis, step):
        size = lax.axis_size(axis)
        return lax.ppermute(value, axis, [(i, (i + step) % size) for i in range(size)])

    xb, xa = move(xl, "stream", 1), move(xf, "stream", -1)
    yb, ya = move(yl, "span", 1), move(yf, "span", -1)
    zb = move(lax.optimization_barrier((zs, xb))[0], "depth", 1)
    za = move(lax.optimization_barrier((zs, xb))[0], "depth", -1)

    wk = pl.pallas_call(
        weights_kernel,
        in_specs=[VMEM],
        out_specs=VMEM,
        out_shape=shape(snaps, DEPTH, dtype=BF16),
        compiler_params=params,
        interpret=INTERPRET,
    )(w)

    span = lax.axis_size("span")
    others = lax.axis_size(("stream", "depth"))
    sh, sl, grams = pl.pallas_call(
        compute_kernel,
        in_specs=[VMEM] * 8,
        out_specs=[VMEM] * 3,
        out_shape=[
            shape(snaps, cells, dtype=BF16),
            shape(snaps, cells, dtype=BF16),
            shape(span, 1, 640),
        ],
        scratch_shapes=[
            pltpu.VMEM((6, planes, rows + 16, cols), F32),
            pltpu.VMEM((18 * planes * rows, cols), F32),
        ],
        compiler_params=params,
        interpret=INTERPRET,
    )(fields, xb, xa, yb, ya, zb, za, wk)

    grams = lax.all_to_all(grams, "span", 0, 0, tiled=True)
    grams = jnp.broadcast_to(grams.sum(0)[None], (others, 1, 640))
    grams = lax.all_to_all(grams, ("stream", "depth"), 0, 0, tiled=True)

    return pl.pallas_call(
        functools.partial(basis_kernel, cells * span * others),
        in_specs=[VMEM] * 3,
        out_specs=HBM,
        out_shape=shape(snaps, planes, rows, cols),
        scratch_shapes=[
            pltpu.VMEM((planes, snaps, rows, cols), F32),
            pltpu.SemaphoreType.DMA((planes,)),
        ],
        compiler_params=params,
        interpret=INTERPRET,
    )(grams, sh, sl)


def solution(mesh):
    spec = P(None, "stream", "span", "depth")
    return jax.shard_map(body, mesh=mesh, in_specs=(spec, spec, P()), out_specs=spec, check_vma=False)
```

```python
import functools

import jax
import jax.numpy as jnp
from jax import lax
from jax.experimental import pallas as pl
from jax.experimental.pallas import tpu as pltpu
from jax.sharding import PartitionSpec as P

F32 = jnp.float32
BF16 = jnp.bfloat16
INTERPRET = False
VMEM = pl.BlockSpec(memory_space=pltpu.VMEM)
HBM = pl.BlockSpec(memory_space=pltpu.HBM)
GROUP = 80
DEPTH = 256
BLOCK = 8


def iota(shape, dim):
    return lax.broadcasted_iota(jnp.int32, shape, dim)


def split(value):
    high = value.astype(BF16)
    low = (value - high.astype(F32)).astype(BF16)
    return high, low


def dot(left, right):
    return jnp.dot(left, right, preferred_element_type=F32)


def dot_nt(left, right):
    return lax.dot_general(left, right, (((1,), (1,)), ((), ())), preferred_element_type=F32)


def place(index):
    return divmod(index * 4, 128)


def sends_kernel(f_hbm, a_hbm, w_hbm, fields, w_ref, xf, xl, yf, yl, zs, sems):
    copies = [
        pltpu.make_async_copy(f_hbm, fields.at[0:3], sems.at[0]),
        pltpu.make_async_copy(a_hbm, fields.at[3:6], sems.at[1]),
        pltpu.make_async_copy(w_hbm, w_ref, sems.at[2]),
    ]
    for copy in copies:
        copy.start()
    for copy in copies:
        copy.wait()
    comps, planes, rows = fields.shape[:3]
    xf[...] = fields[:, 0:2]
    xl[...] = fields[:, planes - 2 : planes]
    yf[...] = fields[:, :, 0:2, :]
    yl[...] = fields[:, :, rows - 2 : rows, :]
    lane = iota((8, 128), 1)
    packed = [jnp.zeros((8, 128), F32) for _ in range(zs.shape[0] // 8)]
    for comp in range(comps):
        for plane in range(planes):
            for half in range(rows // 8):
                group, at = place((comp * planes + plane) * (rows // 8) + half)
                tile = fields[comp, plane, 8 * half : 8 * half + 8, :]
                moved = pltpu.roll(tile, (2 + at) % 128, 1)
                here = (lane >= at) & (lane < at + 4)
                packed[group] = jnp.where(here, moved, packed[group])
    for group, tile in enumerate(packed):
        zs[8 * group : 8 * group + 8, :] = tile


def weights_kernel(w_ref, wk_ref):
    pairs = w_ref.shape[1]
    high, low = split(w_ref[...] * (1.0 / 144.0))
    q = iota((pairs, DEPTH), 1)
    p = iota((pairs, DEPTH), 0)
    r = jnp.where(q >= 2 * GROUP, q - 2 * GROUP, jnp.where(q >= GROUP, q - GROUP, q))
    wanted = jnp.where(r < 72, 9 * lax.shift_right_logical(r, 3) + (r & 7), 9 * (r - 72) + 8)
    wanted = jnp.where(q >= 3 * GROUP, pairs - 1, wanted)
    use_low = ((q >= 2 * GROUP) & (q < 3 * GROUP)) | (q == 3 * GROUP + 2)
    hit = (wanted == p) & (q < 3 * GROUP + 3)
    to_high = jnp.where(hit & ~use_low, 1.0, 0.0).astype(BF16)
    to_low = jnp.where(hit & use_low, 1.0, 0.0).astype(BF16)
    wk_ref[...] = (dot(high, to_high) + dot(low, to_low)).astype(BF16)


def compute_kernel(fields, xb, xa, yb, ya, zb, za, wk_ref, sh_ref, sl_ref, g_ref, ypad, grads):
    planes, rows = fields.shape[1], fields.shape[2]
    halves = rows // 8
    lane = iota((8, 128), 1)
    total = None
    ypad[:, :, 8 : 8 + rows, :] = fields[...]
    ypad[:, :, 6:8, :] = yb[...]
    ypad[:, :, 8 + rows : 10 + rows, :] = ya[...]

    def line(comp, plane):
        if plane < 0:
            return xb[comp, plane + 2]
        if plane >= planes:
            return xa[comp, plane - planes]
        return fields[comp, plane]

    def depth_slope(comp, plane, half):
        tile = fields[comp, plane, 8 * half : 8 * half + 8, :]
        group, at = place((comp * planes + plane) * halves + half)
        before = zb[8 * group : 8 * group + 8, :]
        after = za[8 * group : 8 * group + 8, :]
        up1 = jnp.where(lane < 1, pltpu.roll(before, (127 - at) % 128, 1), pltpu.roll(tile, 1, 1))
        up2 = jnp.where(lane < 2, pltpu.roll(before, (128 - at) % 128, 1), pltpu.roll(tile, 2, 1))
        dn1 = jnp.where(lane >= 127, pltpu.roll(after, (125 - at) % 128, 1), pltpu.roll(tile, 127, 1))
        dn2 = jnp.where(lane >= 126, pltpu.roll(after, (124 - at) % 128, 1), pltpu.roll(tile, 126, 1))
        return 8.0 * (dn1 - up1) - (dn2 - up2)

    lines = planes * rows
    third = iota((16, 128), 0)
    for plane in range(planes):
        for comp in range(6):
            dx = 8.0 * (line(comp, plane + 1) - line(comp, plane - 1)) - (
                line(comp, plane + 2) - line(comp, plane - 2)
            )
            y = lambda k: ypad[comp, plane, 8 + k : 8 + k + rows, :]
            dy = 8.0 * (y(1) - y(-1)) - (y(2) - y(-2))
            dz = jnp.concatenate([depth_slope(comp, plane, h) for h in range(halves)], 0)
            for dim, slope in enumerate((dx, dy, dz)):
                at = (3 * comp + dim) * lines + plane * rows
                grads[at : at + rows, :] = slope
        for first in range(plane * rows, (plane + 1) * rows, 2):
            columns = []
            for at in (first, first + 1):
                one = lambda entry: grads[entry * lines + at : entry * lines + at + 1, :]
                forward = grads[pl.ds(at, 8, stride=lines), :]
                adjoint = grads[pl.ds(9 * lines + at, 8, stride=lines), :]
                products = [one(a) * adjoint for a in range(9)] + [forward * one(17)]
                high, low = split(jnp.concatenate(products, 0))
                final = jnp.broadcast_to(one(8) * one(17), third.shape)
                final_high = final.astype(BF16).astype(F32)
                final = jnp.where(third == 1, final - final_high, final_high)
                final = jnp.where(third < 3, final, 0.0).astype(BF16)
                columns.append(jnp.concatenate([high, low, high, final], 0))
            block = dot(wk_ref[...], jnp.concatenate(columns, 1))
            high, low = split(block)
            sh_ref[:, 128 * first : 128 * first + 256] = high
            sl_ref[:, 128 * first : 128 * first + 256] = low
            both = jnp.concatenate([high, low], 0)
            part = dot_nt(both, jnp.concatenate([both, both], 0))
            total = part if total is None else total + part

    snaps = total.shape[0] // 2
    gram = total[:snaps] + total[snaps:]
    gram = gram + pltpu.roll(gram, snaps, 1)
    row, wide = iota((16, 128), 0), iota((16, 128), 1)
    half = jnp.where(((wide - row) & 31) < 16, gram[0:16], gram[16:32])
    middle = jnp.sum(jnp.where((wide & 31) == row + 16, gram[0:16], 0.0), axis=0, keepdims=True)
    parts = [half[0:8], pltpu.roll(half[0:8], 4, 0), half[8:16], pltpu.roll(half[8:16], 4, 0)]
    packed = parts[0]
    for k in range(1, 4):
        packed = jnp.where(lane >= 32 * k, parts[k], packed)
    for j in range(5):
        line = packed[j : j + 1] if j < 4 else middle
        g_ref[:, :, 128 * j : 128 * j + 128] = jnp.broadcast_to(line[None], (g_ref.shape[0], 1, 128))


def inverse_factor(gram, snaps):
    row, lane = iota(gram.shape, 0), iota(gram.shape, 1)
    work = jnp.where(lane < snaps, gram, jnp.where(lane == row + snaps, 1.0, 0.0))
    for first in range(0, snaps, BLOCK):
        block = range(first, first + BLOCK)
        cols = [jnp.broadcast_to(work[:, k : k + 1], work.shape) for k in block]
        rows = [work[k : k + 1, :] for k in block]
        for i, k in enumerate(block):
            inverse = 1.0 / cols[i][k : k + 1, :]
            below = jnp.where(row > k, cols[i], 0.0)
            scaled = rows[i] * inverse
            work = work - below * scaled
            for j in range(i + 1, BLOCK):
                entry = cols[i][first + j : first + j + 1, :]
                cols[j] = cols[j] - below * (entry * inverse)
                rows[j] = rows[j] - entry * scaled
    diagonal = jnp.sum(jnp.where(lane == row, work, 0.0), axis=1, keepdims=True)
    work = work * (1.0 / jnp.sqrt(diagonal))
    return jnp.where(lane < snaps, pltpu.roll(work, 128 - snaps, 1), 0.0)


def basis_kernel(cells, r_ref, sh_ref, sl_ref, o_hbm, out_ref, sems):
    planes, snaps, rows, cols = out_ref.shape
    packed = r_ref[0]
    for i in range(1, r_ref.shape[0]):
        packed = packed + r_ref[i]
    packed = packed * (1.0 / cells)
    row8 = iota((8, 128), 0)
    quad = jnp.zeros((8, 128), F32)
    for j in range(4):
        quad = jnp.where((row8 & 3) == j, packed[:, 128 * j : 128 * j + 128], quad)
    turned = [quad] + [pltpu.roll(quad, 128 - 32 * k, 1) for k in range(1, 4)]
    half = [jnp.where(row8 < 4, turned[2 * k], turned[2 * k + 1]) for k in range(2)]
    half = jnp.concatenate(half + half, 0)
    row, wide = iota((snaps, 128), 0), iota((snaps, 128), 1)
    middle = (row < 16) & (wide == row + 16)
    half = jnp.where(middle, packed[:, 512:640], half)
    known = (wide < snaps) & (middle | (((wide - row) & 31) < 16))
    half = jnp.where(known, half, 0.0)
    mirror = jnp.concatenate([half, jnp.zeros((128 - snaps, 128), F32)], 0).T[0:snaps]
    gram = jnp.where(known, half, mirror)
    inverse = inverse_factor(gram, snaps)
    high = inverse.astype(BF16).astype(F32)
    low = inverse - high
    factor = high + pltpu.roll(high, snaps, 1)
    factor = factor + pltpu.roll(low, 2 * snaps, 1)
    factor = factor.astype(BF16)[:, 0 : 3 * snaps]

    flat = out_ref.reshape(planes * snaps * rows, cols)
    copies = []
    for plane in range(planes):
        part = slice(plane * rows * cols, (plane + 1) * rows * cols)
        both = jnp.concatenate([sh_ref[:, part], sl_ref[:, part]], 0)
        out = dot(factor, jnp.concatenate([both, sh_ref[:, part]], 0))
        for y in range(rows):
            flat[pl.ds(plane * snaps * rows + y, snaps, stride=rows), :] = out[:, cols * y : cols * y + cols]
        copy = pltpu.make_async_copy(out_ref.at[plane], o_hbm.at[:, plane], sems.at[plane])
        copy.start()
        copies.append(copy)
    for copy in copies:
        copy.wait()


def shape(*dims, dtype=F32):
    return jax.ShapeDtypeStruct(dims, dtype)


def body(forward_velocity, adjoint_velocity, weights):
    _, planes, rows, cols = forward_velocity.shape
    snaps = weights.shape[0]
    cells = planes * rows * cols
    zrows = -(-6 * planes * (rows // 8) * 4 // 128) * 8
    params = pltpu.CompilerParams(vmem_limit_bytes=48 * 2**20)

    fields, w, xf, xl, yf, yl, zs = pl.pallas_call(
        sends_kernel,
        in_specs=[HBM] * 3,
        out_specs=[VMEM] * 7,
        out_shape=[
            shape(6, planes, rows, cols),
            shape(*weights.shape),
            shape(6, 2, rows, cols),
            shape(6, 2, rows, cols),
            shape(6, planes, 2, cols),
            shape(6, planes, 2, cols),
            shape(zrows, 128),
        ],
        scratch_shapes=[pltpu.SemaphoreType.DMA((3,))],
        compiler_params=params,
        interpret=INTERPRET,
    )(*(pltpu.with_memory_space_constraint(x, pltpu.HBM) for x in (forward_velocity, adjoint_velocity, weights)))

    def move(value, axis, step):
        size = lax.axis_size(axis)
        return lax.ppermute(value, axis, [(i, (i + step) % size) for i in range(size)])

    xb, xa = move(xl, "stream", 1), move(xf, "stream", -1)
    yb, ya = move(yl, "span", 1), move(yf, "span", -1)
    zb = move(lax.optimization_barrier((zs, xb))[0], "depth", 1)
    za = move(lax.optimization_barrier((zs, xb))[0], "depth", -1)

    wk = pl.pallas_call(
        weights_kernel,
        in_specs=[VMEM],
        out_specs=VMEM,
        out_shape=shape(snaps, DEPTH, dtype=BF16),
        compiler_params=params,
        interpret=INTERPRET,
    )(w)

    span = lax.axis_size("span")
    others = lax.axis_size(("stream", "depth"))
    sh, sl, grams = pl.pallas_call(
        compute_kernel,
        in_specs=[VMEM] * 8,
        out_specs=[VMEM] * 3,
        out_shape=[
            shape(snaps, cells, dtype=BF16),
            shape(snaps, cells, dtype=BF16),
            shape(span, 1, 640),
        ],
        scratch_shapes=[
            pltpu.VMEM((6, planes, rows + 16, cols), F32),
            pltpu.VMEM((18 * planes * rows, cols), F32),
        ],
        compiler_params=params,
        interpret=INTERPRET,
    )(fields, xb, xa, yb, ya, zb, za, wk)

    grams = lax.all_to_all(grams, "span", 0, 0, tiled=True)
    grams = jnp.broadcast_to(grams.sum(0)[None], (others, 1, 640))
    grams = lax.all_to_all(grams, ("stream", "depth"), 0, 0, tiled=True)

    return pl.pallas_call(
        functools.partial(basis_kernel, cells * span * others),
        in_specs=[VMEM] * 3,
        out_specs=HBM,
        out_shape=shape(snaps, planes, rows, cols),
        scratch_shapes=[
            pltpu.VMEM((planes, snaps, rows, cols), F32),
            pltpu.SemaphoreType.DMA((planes,)),
        ],
        compiler_params=params,
        interpret=INTERPRET,
    )(grams, sh, sl)


def solution(mesh):
    spec = P(None, "stream", "span", "depth")
    return jax.shard_map(body, mesh=mesh, in_specs=(spec, spec, P()), out_specs=spec, check_vma=False)
```
